256 devices in a mesh: row: 8 (over x, z_lo), col: 32 (over y, z_hi, core).
Axes of the slice: x: 4, y: 4, z: 8 (z_hi: 4, z_lo: 2; z = z_hi * 2 + z_lo), core: 2. Of those that a mesh axis runs over, the one named last changes fastest.
Arguments:
- activations: bfloat16 [1024, 8192], P('col', 'row'), may hold values from -6 to 6
- up_weight: bfloat16 [8192, 53248], P('row', 'col'), may hold values from -0.0625 to 0.0625
- out_grad: bfloat16 [1024, 53248], P('row', 'col'), may hold values from -6 to 6
- round_seed: int32 [1], replicated, may hold values from 0 to 1073741823
- counter_base: int32 [1024], P('row'), may hold values from 0 to 1073741823
Outputs:
- weight_grad: float32 [8192, 53248], P('row', 'col')
- input_grad: bfloat16 [1024, 8192], P('col', 'row')
The draws below stay inside these ranges and needn't reach their ends.
All inputs are finite; a program needn't handle non-finite values.
Results may differ from the reference program's by a relative error of at most 0.015.
Values may be sent and summed in bfloat16 or wider, within the bound.
A program may use at most 64 MiB of HBM per device.

```python
import jax
import jax.numpy as jnp
from jax import lax

D = 8192
FF = 53248
TOKENS = 1024
FF_BLOCK = 1664
N_COL = 32


def touch_ends(drawn, key, least, largest):
    longest = drawn.shape.index(max(drawn.shape))
    spots = []
    for shift in (0, 1):
        where = [jax.random.randint(jax.random.fold_in(key, axis), (), 0, length) for axis, length in enumerate(drawn.shape)]
        where[longest] = (where[longest] + shift) % drawn.shape[longest]
        spots.append(tuple(where))
    return drawn.at[spots[0]].set(least).at[spots[1]].set(largest)


def level_of(own_key, shape, split, smallest, largest):
    factor_of = 1.0
    for position, blocks in split:
        steps = jax.random.uniform(jax.random.fold_in(jax.random.fold_in(own_key, 6), position), (blocks,), jnp.float32, smallest / len(split), largest / len(split))
        factor_of = factor_of * jnp.repeat(jnp.exp(steps), shape[position] // blocks).reshape((-1,) + (1,) * (len(shape) - 1 - position))
    return factor_of


def noise(stream_key, extent, deviation, most, shards=(), kind=jnp.bfloat16):
    values = deviation * jax.random.normal(stream_key, extent, jnp.float32)
    if shards:
        values = values * level_of(stream_key, extent, shards, -0.22, 0.18)
    return jnp.clip(values, -most, most).astype(kind)


def setup_inputs(seed: int = 0) -> dict:
    key_list = jax.random.split(jax.random.key(seed), 6)
    return {
        "activations": noise(key_list[0], (TOKENS, D), 1.0, 6.0, ((0, 32), (1, 8))),
        "up_weight": noise(key_list[1], (D, FF), D ** -0.5, 0.0625, ((0, 8), (1, 32))),
        "out_grad": noise(key_list[2], (TOKENS, FF), 1.0, 6.0, ((0, 8), (1, 32))),
        "round_seed": jax.random.randint(key_list[3], (1,), 0, 1073741824).astype(jnp.int32),
        "counter_base": touch_ends(jax.random.randint(key_list[4], (TOKENS,), 0, 1073741824), jax.random.fold_in(key_list[4], 1), 0, 1073741823).astype(jnp.int32),
    }


def stochastic_round(grad, counter_base, round_seed, col_first):
    columns = col_first + lax.broadcasted_iota(jnp.int32, grad.shape, 1)
    counter = counter_base[:, None] + columns
    mixed = counter * jnp.int32(747796405) + round_seed[0] * jnp.int32(1013904223)
    mixed = mixed ^ (mixed >> 15)
    mixed = mixed * jnp.int32(277803737)
    mixed = mixed ^ (mixed >> 16)
    level = (mixed & 255).astype(jnp.float32)
    scaled = grad.astype(jnp.float32) * 4.0 + (level + 0.5) / 256.0
    return (jnp.floor(scaled) / 4.0).astype(jnp.bfloat16)


def reference(activations, up_weight, out_grad, round_seed, counter_base):
    quantized = stochastic_round(out_grad, counter_base, round_seed, 0)
    weight_grad = jnp.dot(activations.T, quantized, preferred_element_type=jnp.float32) * (TOKENS ** -0.5)

    def add_block(block, total):
        offset = (block * FF_BLOCK).astype(jnp.int32)
        grad_rows = lax.dynamic_slice_in_dim(quantized, offset, FF_BLOCK, 1)
        weight_cols = lax.dynamic_slice_in_dim(up_weight, offset, FF_BLOCK, 1)
        partial_value = jnp.dot(grad_rows, weight_cols.T, preferred_element_type=jnp.float32).astype(jnp.bfloat16)
        partial_value = lax.optimization_barrier(partial_value)
        return total + partial_value.astype(jnp.float32)

    summed = lax.fori_loop(0, N_COL, add_block, jnp.zeros((TOKENS, D), jnp.float32))
    return weight_grad, summed.astype(jnp.bfloat16)
```

```python
import functools

import jax
import jax.numpy as jnp
from jax import lax
from jax.experimental import pallas as pl
from jax.experimental.pallas import tpu as pltpu
from jax.sharding import PartitionSpec as P

MESH = pl.DeviceIdType.MESH
NX, NY, NH = 4, 4, 4
OWN, LEFT, RIGHT, FAR, OWN2, LEFT2, RIGHT2, FAR2 = range(8)
SHARDS = ((0, 0), (3, 0), (1, 0), (2, 0), (0, 1), (3, 1), (1, 1), (2, 1))


def place():
    row, col = lax.axis_index("row"), lax.axis_index("col")
    return lax.div(row, 2), lax.rem(row, 2), lax.div(col, 8), lax.rem(lax.div(col, 2), 4), lax.rem(col, 2)


def device(x, lo, y, hi, core):
    return (x * 2 + lo, (y * NH + hi) * 2 + core)


def exchange_kernel(
    act_hbm, weight_hbm, grad_hbm, seed_ref, base_ref, g_ref, a_ref, out_ref,
    grad, weight, part, crecv, ssum, yrecv, tsum, zrecv,
    lsem, gs, gr, cs, cr, ys, yr, zs, zr, azs, azr, ays, ayr, acs, acr,
):
    x, lo, y, hi, core = place()
    tokens, ff = grad.shape
    block = tokens // 4
    my_slot = x * 2 + lo
    here = device(x, lo, y, hi, core)
    right = device(lax.rem(x + 1, NX), lo, y, hi, core)
    left = device(lax.rem(x + 3, NX), lo, y, hi, core)
    pair = device(x, 1 - lo, y, hi, core)
    sibling = device(x, lo, y, hi, 1 - core)

    def at_y(yy):
        return device(x, lo, yy, hi, core)

    def at_hi(hh):
        return device(x, lo, y, hh, core)

    def slot(i):
        dx, other = SHARDS[i]
        return lax.rem(x + dx, NX) * 2 + lax.rem(lo + other, 2)

    load_grad = pltpu.make_async_copy(grad_hbm, grad, lsem.at[0])
    load_grad.start()
    load_weight = pltpu.make_async_copy(weight_hbm, weight, lsem.at[1])
    load_weight.start()
    load_act = pltpu.make_async_copy(act_hbm, a_ref.at[y, hi, core], lsem.at[2])
    load_act.start()

    barrier = pltpu.get_barrier_semaphore()
    peers = [right, left, pair, sibling]
    peers += [at_y(lax.rem(y + d, NY)) for d in (1, 2, 3)]
    peers += [at_hi(lax.rem(hi + d, NH)) for d in (1, 2, 3)]
    for peer in peers:
        pl.semaphore_signal(barrier, inc=1, device_id=peer, device_id_type=MESH)

    load_grad.wait()
    base = jnp.transpose(jnp.broadcast_to(base_ref[...], (tokens, tokens)))
    mixed_seed = seed_ref[0] * jnp.int32(1013904223)
    first = lax.axis_index("col") * ff

    def round_columns(n, _):
        columns = pl.ds(pl.multiple_of(n * 128, 128), 128)
        counter = base + (first + n * 128 + lax.broadcasted_iota(jnp.int32, (tokens, 128), 1))
        mixed = counter * jnp.int32(747796405) + mixed_seed
        mixed = mixed ^ (mixed >> 15)
        mixed = mixed * jnp.int32(277803737)
        mixed = mixed ^ (mixed >> 16)
        level = (mixed & 255).astype(jnp.float32)
        scaled = grad[:, columns].astype(jnp.float32) * 4.0 + (level + 0.5) / 256.0
        rounded = (jnp.floor(scaled) / 4.0).astype(jnp.bfloat16)
        g_ref[my_slot, :, :, columns] = rounded.reshape(4, block, 128)
        return 0

    lax.fori_loop(0, ff // 128, round_columns, 0)
    pl.semaphore_wait(barrier, len(peers))

    sends = []

    def send_g(i, j, to):
        where = g_ref.at[slot(i), j]
        copy = pltpu.make_async_remote_copy(
            src_ref=where, dst_ref=where, send_sem=gs.at[len(sends)], recv_sem=gr.at[slot(i), j],
            device_id=to, device_id_type=MESH,
        )
        copy.start()
        sends.append(copy)

    def wait_g(i, *js):
        for j in js:
            where = g_ref.at[slot(i), j]
            pltpu.make_async_remote_copy(
                src_ref=where, dst_ref=where, send_sem=gs.at[0], recv_sem=gr.at[slot(i), j],
                device_id=here, device_id_type=MESH,
            ).wait_recv()

    def core_copy(i):
        return pltpu.make_async_remote_copy(
            src_ref=part.at[i, :, 1 - core], dst_ref=crecv.at[i], send_sem=cs.at[i], recv_sem=cr.at[i],
            device_id=sibling, device_id_type=MESH,
        )

    def project(i):
        where = slot(i)

        def features(n, _):
            wide = pl.ds(pl.multiple_of(n * 256, 256), 256)
            value = lax.dot_general(
                g_ref[where].reshape(tokens, ff), weight[wide, :], (((1,), (1,)), ((), ())),
                preferred_element_type=jnp.float32,
            )
            part[i, :, :, :, wide] = value.astype(jnp.bfloat16).reshape(2, 2, block, 256)
            return 0

        lax.fori_loop(0, weight.shape[0] // 256, features, 0)
        core_copy(i).start()

    def root(i):
        return lax.rem(x + SHARDS[i][0], NX)

    def y_copy(i):
        to = root(i)
        lo_root = lax.rem(lo + SHARDS[i][1], 2)
        k = lax.rem(y + NY - to, NY) - 1
        return pltpu.make_async_remote_copy(
            src_ref=ssum.at[i], dst_ref=yrecv.at[lo_root, k], send_sem=ys.at[i], recv_sem=yr.at[lo_root, k],
            device_id=at_y(to), device_id_type=MESH,
        )

    def add_cores(i):
        core_copy(i).wait_recv()
        ssum[i] = (part[i, :, core].astype(jnp.float32) + crecv[i].astype(jnp.float32)).astype(jnp.bfloat16)

        @pl.when(y != root(i))
        def _():
            y_copy(i).start()

    def z_copy(lo_root, q):
        to = 2 * lo_root + q
        k = lax.rem(hi + NH - to, NH) - 1
        return pltpu.make_async_remote_copy(
            src_ref=tsum.at[lo_root, q], dst_ref=zrecv.at[k], send_sem=zs.at[lo_root, q], recv_sem=zr.at[k],
            device_id=at_hi(to), device_id_type=MESH,
        )

    def add_columns(i):
        @pl.when(y == root(i))
        def _():
            lo_root = lax.rem(lo + SHARDS[i][1], 2)
            total = ssum[i].astype(jnp.float32)
            for k in range(3):
                pltpu.make_async_remote_copy(
                    src_ref=ssum.at[i], dst_ref=yrecv.at[lo_root, k], send_sem=ys.at[i], recv_sem=yr.at[lo_root, k],
                    device_id=here, device_id_type=MESH,
                ).wait_recv()
                total += yrecv[lo_root, k].astype(jnp.float32)
            tsum[lo_root] = total.astype(jnp.bfloat16)
            for q in range(2):

                @pl.when(hi != 2 * lo_root + q)
                def _():
                    z_copy(lo_root, q).start()

    def az_copy(d):
        where = a_ref.at[y, hi, core]
        return pltpu.make_async_remote_copy(
            src_ref=where, dst_ref=where, send_sem=azs.at[d - 1], recv_sem=azr.at[d - 1],
            device_id=at_hi(lax.rem(hi + d, NH)), device_id_type=MESH,
        )

    def ay_copy(d):
        where = a_ref.at[y, :, core]
        return pltpu.make_async_remote_copy(
            src_ref=where, dst_ref=where, send_sem=ays.at[d - 1], recv_sem=ayr.at[d - 1],
            device_id=at_y(lax.rem(y + d, NY)), device_id_type=MESH,
        )

    def ac_copy(d):
        where = a_ref.at[lax.rem(y + NY - d, NY), :, core]
        return pltpu.make_async_remote_copy(
            src_ref=where, dst_ref=where, send_sem=acs.at[d], recv_sem=acr.at[d],
            device_id=sibling, device_id_type=MESH,
        )

    def az_wait(d):
        where = a_ref.at[y, lax.rem(hi + NH - d, NH), core]
        pltpu.make_async_remote_copy(
            src_ref=where, dst_ref=where, send_sem=azs.at[d - 1], recv_sem=azr.at[d - 1],
            device_id=here, device_id_type=MESH,
        ).wait_recv()

    def ay_wait(d):
        where = a_ref.at[lax.rem(y + NY - d, NY), :, core]
        pltpu.make_async_remote_copy(
            src_ref=where, dst_ref=where, send_sem=ays.at[d - 1], recv_sem=ayr.at[d - 1],
            device_id=here, device_id_type=MESH,
        ).wait_recv()

    def ac_wait(d):
        where = a_ref.at[lax.rem(y + NY - d, NY), :, 1 - core]
        pltpu.make_async_remote_copy(
            src_ref=where, dst_ref=where, send_sem=acs.at[d], recv_sem=acr.at[d],
            device_id=here, device_id_type=MESH,
        ).wait_recv()

    for j, k, p in ((0, 3, 0), (1, 2, 3), (2, 1, 1), (3, 0, 2)):
        send_g(OWN, j, right)
        send_g(OWN, k, left)
        send_g(OWN, p, pair)
    load_weight.wait()
    project(OWN)
    wait_g(LEFT, 0)
    send_g(LEFT, 0, right)
    wait_g(RIGHT, 3)
    send_g(RIGHT, 3, left)
    add_cores(OWN)
    wait_g(LEFT, 1)
    send_g(LEFT, 1, right)
    wait_g(RIGHT, 2)
    send_g(RIGHT, 2, left)
    wait_g(OWN2, 0)
    send_g(OWN2, 0, right)
    wait_g(OWN2, 3)
    send_g(OWN2, 3, left)
    wait_g(OWN2, 1)
    send_g(OWN2, 1, right)
    wait_g(OWN2, 2)
    send_g(OWN2, 2, left)
    for j, k in ((2, 1), (3, 0)):
        send_g(OWN2, j, right)
        send_g(OWN2, k, left)
    load_act.wait()
    for d in (1, 2, 3):
        az_copy(d).start()
    wait_g(LEFT, 2, 3)
    project(LEFT)
    wait_g(RIGHT, 1, 0)
    project(RIGHT)
    project(OWN2)
    add_columns(OWN)
    add_cores(LEFT)
    add_cores(RIGHT)
    add_cores(OWN2)
    for d in (1, 2, 3):
        az_wait(d)
    for d in (1, 2, 3):
        ay_copy(d).start()
    ac_copy(0).start()
    wait_g(FAR, 0, 3, 1, 2)
    project(FAR)
    add_columns(LEFT)
    add_columns(RIGHT)
    add_columns(OWN2)
    add_cores(FAR)
    wait_g(LEFT2, 0)
    send_g(LEFT2, 0, right)
    wait_g(RIGHT2, 3)
    send_g(RIGHT2, 3, left)
    wait_g(LEFT2, 1)
    send_g(LEFT2, 1, right)
    wait_g(RIGHT2, 2)
    send_g(RIGHT2, 2, left)
    add_columns(FAR)
    for d in (1, 2, 3):
        ay_wait(d)
        ac_copy(d).start()
    wait_g(LEFT2, 2, 3)
    project(LEFT2)
    wait_g(RIGHT2, 1, 0)
    project(RIGHT2)
    add_cores(LEFT2)
    add_cores(RIGHT2)
    wait_g(FAR2, 0, 3, 1, 2)
    project(FAR2)
    add_columns(LEFT2)
    add_columns(RIGHT2)
    add_cores(FAR2)
    add_columns(FAR2)
    for d in range(4):
        ac_wait(d)

    own_lo, own_q = lax.div(hi, 2), lax.rem(hi, 2)
    total = tsum[own_lo, own_q].astype(jnp.float32)
    for k in range(3):
        pltpu.make_async_remote_copy(
            src_ref=zrecv.at[k], dst_ref=zrecv.at[k], send_sem=zs.at[0, 0], recv_sem=zr.at[k],
            device_id=here, device_id_type=MESH,
        ).wait_recv()
        total += zrecv[k].astype(jnp.float32)
    out_ref[...] = total.astype(jnp.bfloat16)

    for copy in sends:
        copy.wait_send()
    for i in range(8):
        core_copy(i).wait_send()

        @pl.when(y != root(i))
        def _():
            y_copy(i).wait_send()

        @pl.when(y == root(i))
        def _():
            lo_root = lax.rem(lo + SHARDS[i][1], 2)
            for q in range(2):

                @pl.when(hi != 2 * lo_root + q)
                def _():
                    z_copy(lo_root, q).wait_send()

    for d in (1, 2, 3):
        az_copy(d).wait_send()
        ay_copy(d).wait_send()
    for d in range(4):
        ac_copy(d).wait_send()


def shards(activations, up_weight, out_grad, round_seed, counter_base):
    tokens, ff = out_grad.shape
    few, features = activations.shape
    all_tokens = few * lax.axis_size("col")
    bf16, dma = jnp.bfloat16, pltpu.SemaphoreType.DMA
    vmem, anywhere = pl.BlockSpec(memory_space=pltpu.VMEM), pl.BlockSpec(memory_space=pl.ANY)
    g, a, input_grad = pl.pallas_call(
        exchange_kernel,
        out_shape=(
            pltpu.VMEM((8, 4, tokens // 4, ff), bf16),
            pltpu.VMEM((NY, NH, 2, few, features), bf16),
            jax.ShapeDtypeStruct((few, features), bf16),
        ),
        in_specs=[anywhere, anywhere, anywhere, pl.BlockSpec(memory_space=pltpu.SMEM), vmem],
        out_specs=(vmem, vmem, vmem),
        scratch_shapes=[
            pltpu.VMEM((tokens, ff), bf16),
            pltpu.VMEM((features, ff), bf16),
            pltpu.VMEM((8, 2, 2, few, features), bf16),
            pltpu.VMEM((8, 2, few, features), bf16),
            pltpu.VMEM((8, 2, few, features), bf16),
            pltpu.VMEM((2, 3, 2, few, features), bf16),
            pltpu.VMEM((2, 2, few, features), bf16),
            pltpu.VMEM((3, few, features), bf16),
            dma((3,)), dma((28,)), dma((8, 4)), dma((8,)), dma((8,)), dma((8,)), dma((2, 3)),
            dma((2, 2)), dma((3,)), dma((3,)), dma((3,)), dma((3,)), dma((3,)), dma((4,)), dma((4,)),
        ],
        compiler_params=pltpu.CompilerParams(
            collective_id=0, has_side_effects=True, vmem_limit_bytes=48 * 1024 * 1024
        ),
        name="exchange",
    )(activations, up_weight, out_grad, round_seed, counter_base.reshape(1, tokens))
    weight_grad = lax.dot_general(
        a.reshape(all_tokens, features), g.reshape(all_tokens, ff), (((0,), (0,)), ((), ())),
        preferred_element_type=jnp.float32,
    )
    return weight_grad * all_tokens ** (-0.5), input_grad


def solution(mesh):
    placed = (P("col", "row"), P("row", "col"), P("row", "col"), P(), P("row"))
    return jax.shard_map(
        shards,
        mesh=mesh,
        in_specs=placed,
        out_specs=(P("row", "col"), P("col", "row")),
        check_vma=False,
    )
```

```python
import jax
import jax.numpy as jnp
from jax import lax
from jax.experimental import pallas as pl
from jax.experimental.pallas import tpu as pltpu
from jax.sharding import PartitionSpec as P

MESH = pl.DeviceIdType.MESH
NX, NY, NH = 4, 4, 4
OWN, LEFT, RIGHT, FAR, OWN2, LEFT2, RIGHT2, FAR2 = range(8)
SHARDS = ((0, 0), (3, 0), (1, 0), (2, 0), (0, 1), (3, 1), (1, 1), (2, 1))
WIDE = 512


def device(x, lo, y, hi, core):
    return (x * 2 + lo, (y * NH + hi) * 2 + core)


def exchange_kernel(
    act_hbm, weight_hbm, grad_hbm, base_hbm, seed_ref, total_ref, out_ref,
    g_ref, a_ref, grad, weight, turned, turned_act, base_row, part, crecv, ssum, yrecv, tsum, zrecv,
    lsem, gs, gr, cs, cr, ys, yr, zs, zr, azs, azr, ays, ayr, acs, acr,
):
    row, col = lax.axis_index("row"), lax.axis_index("col")
    x, lo = lax.div(row, 2), lax.rem(row, 2)
    y, hi, core = lax.div(col, 8), lax.rem(lax.div(col, 2), 4), lax.rem(col, 2)
    tokens, ff = grad.shape
    features = weight.shape[0]
    block = tokens // 4
    here = device(x, lo, y, hi, core)
    right = device(lax.rem(x + 1, NX), lo, y, hi, core)
    left = device(lax.rem(x + 3, NX), lo, y, hi, core)
    pair = device(x, 1 - lo, y, hi, core)
    sibling = device(x, lo, y, hi, 1 - core)

    def at_y(yy):
        return device(x, lo, yy, hi, core)

    def at_hi(hh):
        return device(x, lo, y, hh, core)

    def lo_of(i):
        return lax.rem(lo + SHARDS[i][1], 2)

    def root(i):
        return lax.rem(x + SHARDS[i][0], NX)

    def slot(i):
        return root(i) * 2 + lo_of(i)

    def remote(src, dst, send, recv, to):
        return pltpu.make_async_remote_copy(
            src_ref=src, dst_ref=dst, send_sem=send, recv_sem=recv, device_id=to, device_id_type=MESH
        )

    loads = [
        pltpu.make_async_copy(base_hbm, base_row, lsem.at[0]),
        pltpu.make_async_copy(grad_hbm, grad, lsem.at[1]),
        pltpu.make_async_copy(act_hbm, a_ref.at[y, hi, core], lsem.at[2]),
        pltpu.make_async_copy(weight_hbm, weight, lsem.at[3]),
    ]
    for load in loads:
        load.start()

    barrier = pltpu.get_barrier_semaphore()
    peers = [right, left, pair, sibling]
    peers += [at_y(lax.rem(y + d, NY)) for d in (1, 2, 3)]
    peers += [at_hi(lax.rem(hi + d, NH)) for d in (1, 2, 3)]
    for peer in peers:
        pl.semaphore_signal(barrier, inc=1, device_id=peer, device_id_type=MESH)

    for load in loads[:3]:
        load.wait()
    base = jnp.transpose(jnp.broadcast_to(base_row[...], (tokens, tokens)))
    mixed_seed = seed_ref[0] * jnp.int32(1013904223)
    first = col * ff

    def round_columns(n, _):
        columns = pl.ds(pl.multiple_of(n * 128, 128), 128)
        counter = base + (first + n * 128 + lax.broadcasted_iota(jnp.int32, (tokens, 128), 1))
        mixed = counter * jnp.int32(747796405) + mixed_seed
        mixed = mixed ^ (mixed >> 15)
        mixed = mixed * jnp.int32(277803737)
        mixed = mixed ^ (mixed >> 16)
        level = (mixed & 255).astype(jnp.float32)
        scaled = grad[:, columns].astype(jnp.float32) * 4.0 + (level + 0.5) / 256.0
        rounded = (jnp.floor(scaled) / 4.0).astype(jnp.bfloat16)
        g_ref[slot(OWN), :, :, columns] = rounded.reshape(4, block, 128)
        return 0

    lax.fori_loop(0, ff // 128, round_columns, 0)
    pl.semaphore_wait(barrier, len(peers))

    sends = []

    def send_g(i, j, to):
        where = g_ref.at[slot(i), j]
        copy = remote(where, where, gs.at[len(sends)], gr.at[slot(i), j], to)
        copy.start()
        sends.append(copy)

    def wait_g(i, *js):
        for j in js:
            where = g_ref.at[slot(i), j]
            remote(where, where, gs.at[0], gr.at[slot(i), j], here).wait_recv()

    def core_copy(i, q):
        return remote(part.at[i, q, 1 - core], crecv.at[i, q], cs.at[i, q], cr.at[i, q], sibling)

    def project(*units):
        rows = 2 * block

        def step(n, _):
            wide = pl.ds(pl.multiple_of(n * WIDE, WIDE), WIDE)
            left_side = jnp.concatenate(
                [g_ref[slot(i), pl.ds(2 * q, 2)].reshape(rows, ff) for i, q in units], axis=0
            )
            value = lax.dot_general(
                left_side, turned[:, wide], (((1,), (0,)), ((), ())), preferred_element_type=jnp.float32
            ).astype(jnp.bfloat16)
            for u, (i, q) in enumerate(units):
                part[i, q, :, :, wide] = value[u * rows : (u + 1) * rows].reshape(2, block, WIDE)
            return 0

        lax.fori_loop(0, features // WIDE, step, 0)
        for i, q in units:
            core_copy(i, q).start()

    def y_copy(i, q):
        k = lax.rem(y + NY - root(i), NY) - 1
        return remote(ssum.at[i, q], yrecv.at[lo_of(i), k, q], ys.at[i, q], yr.at[lo_of(i), k, q], at_y(root(i)))

    def add_cores(*units):
        for i, q in units:
            core_copy(i, q).wait_recv()
            ssum[i, q] = (part[i, q, core].astype(jnp.float32) + crecv[i, q].astype(jnp.float32)).astype(jnp.bfloat16)

            @pl.when(y != root(i))
            def _():
                y_copy(i, q).start()

    def z_copy(lo_root, q):
        to = 2 * lo_root + q
        k = lax.rem(hi + NH - to, NH) - 1
        return remote(tsum.at[lo_root, q], zrecv.at[k], zs.at[lo_root, q], zr.at[k], at_hi(to))

    def add_columns(*units):
        for i, q in units:

            @pl.when(y == root(i))
            def _():
                lo_root = lo_of(i)
                total = ssum[i, q].astype(jnp.float32)
                for k in range(3):
                    where = yrecv.at[lo_root, k, q]
                    remote(where, where, ys.at[i, q], yr.at[lo_root, k, q], here).wait_recv()
                    total += yrecv[lo_root, k, q].astype(jnp.float32)
                tsum[lo_root, q] = total.astype(jnp.bfloat16)

                @pl.when(hi != 2 * lo_root + q)
                def _():
                    z_copy(lo_root, q).start()

    def az_copy(d):
        where = a_ref.at[y, hi, core]
        return remote(where, where, azs.at[d - 1], azr.at[d - 1], at_hi(lax.rem(hi + d, NH)))

    def az_wait(d):
        where = a_ref.at[y, lax.rem(hi + NH - d, NH), core]
        remote(where, where, azs.at[d - 1], azr.at[d - 1], here).wait_recv()

    def ay_copy(d):
        where = a_ref.at[y, :, core]
        return remote(where, where, ays.at[d - 1], ayr.at[d - 1], at_y(lax.rem(y + d, NY)))

    def ay_wait(d):
        where = a_ref.at[lax.rem(y + NY - d, NY), :, core]
        remote(where, where, ays.at[d - 1], ayr.at[d - 1], here).wait_recv()

    def ac_copy(d):
        where = a_ref.at[lax.rem(y + NY - d, NY), :, core]
        return remote(where, where, acs.at[d], acr.at[d], sibling)

    def ac_wait(d):
        where = a_ref.at[lax.rem(y + NY - d, NY), :, 1 - core]
        remote(where, where, acs.at[d], acr.at[d], here).wait_recv()

    def turn_act(plane):
        for r in range(NX):
            rows = a_ref[r, pl.ds(2 * plane, 2)].reshape(tokens, features)
            turned_act[:, r * tokens : (r + 1) * tokens] = jnp.transpose(rows)

    def accumulate(plane, lowest, highest, last):
        for r in range(0, features, 256):
            value = jnp.zeros((256, highest - lowest), jnp.float32)
            for k in range(NX):
                value += lax.dot_general(
                    turned_act[r : r + 256, k * tokens : (k + 1) * tokens],
                    g_ref[2 * k + plane, :, :, lowest:highest].reshape(tokens, highest - lowest),
                    (((1,), (0,)), ((), ())),
                    preferred_element_type=jnp.float32,
                )
            if last:
                value = (total_ref[r : r + 256, lowest:highest] + value) * (NX * 2 * tokens) ** (-0.5)
            total_ref[r : r + 256, lowest:highest] = value

    spans = [(n, min(n + 512, ff)) for n in range(0, ff, 512)]

    for d in (1, 2, 3):
        az_copy(d).start()
    for j, k, p in ((0, 3, 0), (1, 2, 3), (2, 1, 1), (3, 0, 2)):
        send_g(OWN, j, right)
        send_g(OWN, k, left)
        send_g(OWN, p, pair)
    loads[3].wait()

    def turn_weight(n, _):
        some = pl.ds(pl.multiple_of(n * 128, 128), 128)
        turned[:, some] = jnp.transpose(weight[some, :])
        return 0

    lax.fori_loop(0, features // 128, turn_weight, 0)
    project((OWN, 0), (OWN, 1))
    wait_g(LEFT, 0)
    send_g(LEFT, 0, right)
    wait_g(RIGHT, 3)
    send_g(RIGHT, 3, left)
    add_cores((OWN, 0), (OWN, 1))
    wait_g(LEFT, 1)
    send_g(LEFT, 1, right)
    wait_g(RIGHT, 2)
    send_g(RIGHT, 2, left)
    for d in (1, 2, 3):
        az_wait(d)
    for d in (1, 2, 3):
        ay_copy(d).start()
    ac_copy(0).start()
    wait_g(OWN2, 0)
    send_g(OWN2, 0, right)
    wait_g(OWN2, 3)
    send_g(OWN2, 3, left)
    wait_g(LEFT, 2, 3)
    wait_g(RIGHT, 1, 0)
    project((LEFT, 0), (LEFT, 1), (RIGHT, 0), (RIGHT, 1))
    wait_g(OWN2, 1)
    send_g(OWN2, 1, right)
    wait_g(OWN2, 2)
    send_g(OWN2, 2, left)
    for j, k in ((2, 1), (3, 0)):
        send_g(OWN2, j, right)
        send_g(OWN2, k, left)
    add_cores((LEFT, 0), (LEFT, 1), (RIGHT, 0), (RIGHT, 1))
    wait_g(FAR, 0, 3)
    send_g(FAR, 0, pair)
    send_g(FAR, 3, pair)
    add_columns((OWN, 0), (OWN, 1))
    wait_g(FAR, 1, 2)
    send_g(FAR, 1, pair)
    send_g(FAR, 2, pair)
    project((OWN2, 0), (OWN2, 1), (FAR, 0), (FAR, 1))
    add_cores((OWN2, 0), (OWN2, 1), (FAR, 0), (FAR, 1))
    for d in (1, 2, 3):
        ay_wait(d)
        ac_copy(d).start()
    add_columns((LEFT, 0), (LEFT, 1), (RIGHT, 0), (RIGHT, 1))
    wait_g(LEFT2, 0, 1)
    wait_g(RIGHT2, 3, 2)
    project((LEFT2, 0), (RIGHT2, 1))
    for d in range(4):
        ac_wait(d)
    add_cores((LEFT2, 0), (RIGHT2, 1))
    turn_act(lo)
    for span in spans:
        accumulate(lo, *span, False)
    add_columns((OWN2, 0), (OWN2, 1), (FAR, 0), (FAR, 1))
    turn_act(1 - lo)
    wait_g(LEFT2, 2, 3)
    wait_g(RIGHT2, 1, 0)
    wait_g(FAR2, 0, 3, 1, 2)
    project((LEFT2, 1), (RIGHT2, 0), (FAR2, 0), (FAR2, 1))
    accumulate(1 - lo, *spans[0], True)
    add_cores((LEFT2, 1), (RIGHT2, 0), (FAR2, 0), (FAR2, 1))
    for span in spans[1:3]:
        accumulate(1 - lo, *span, True)
    add_columns((LEFT2, 0), (RIGHT2, 1), (LEFT2, 1), (RIGHT2, 0), (FAR2, 0), (FAR2, 1))
    for span in spans[3:]:
        accumulate(1 - lo, *span, True)

    total = tsum[lax.div(hi, 2), lax.rem(hi, 2)].astype(jnp.float32)
    for k in range(3):
        remote(zrecv.at[k], zrecv.at[k], zs.at[0, 0], zr.at[k], here).wait_recv()
        total += zrecv[k].astype(jnp.float32)
    out_ref[...] = total.astype(jnp.bfloat16)

    for copy in sends:
        copy.wait_send()
    for i in range(8):
        for q in range(2):
            core_copy(i, q).wait_send()

            @pl.when(y != root(i))
            def _():
                y_copy(i, q).wait_send()

            @pl.when((y == root(i)) & (hi != 2 * lo_of(i) + q))
            def _():
                z_copy(lo_of(i), q).wait_send()

    for d in (1, 2, 3):
        az_copy(d).wait_send()
        ay_copy(d).wait_send()
    for d in range(4):
        ac_copy(d).wait_send()


def store_kernel(total_ref, rows_ref, total_hbm, rows_hbm, sem):
    pieces = 8
    step = total_ref.shape[0] // pieces
    copies = [pltpu.make_async_copy(rows_ref, rows_hbm, sem.at[pieces])]
    for n in range(pieces):
        some = pl.ds(n * step, step)
        copies.append(pltpu.make_async_copy(total_ref.at[some], total_hbm.at[some], sem.at[n]))
    for copy in copies:
        copy.start()
    for copy in copies:
        copy.wait()


def shards(activations, up_weight, out_grad, round_seed, counter_base):
    tokens, ff = out_grad.shape
    few, features = activations.shape
    bf16, f32, dma = jnp.bfloat16, jnp.float32, pltpu.SemaphoreType.DMA
    vmem, hbm = pl.BlockSpec(memory_space=pltpu.VMEM), pl.BlockSpec(memory_space=pltpu.HBM)
    operands = (activations, up_weight, out_grad, counter_base.reshape(1, tokens))
    held = [pltpu.with_memory_space_constraint(v, pltpu.HBM) for v in operands]
    total, input_rows = pl.pallas_call(
        exchange_kernel,
        out_shape=(pltpu.VMEM((features, ff), f32), pltpu.VMEM((few, features), bf16)),
        in_specs=[hbm] * 4 + [pl.BlockSpec(memory_space=pltpu.SMEM)],
        out_specs=(vmem, vmem),
        scratch_shapes=[
            pltpu.VMEM((8, 4, tokens // 4, ff), bf16),
            pltpu.VMEM((NY, NH, 2, few, features), bf16),
            pltpu.VMEM((tokens, ff), bf16),
            pltpu.VMEM((features, ff), bf16),
            pltpu.VMEM((ff, features), bf16),
            pltpu.VMEM((features, NX * tokens), bf16),
            pltpu.VMEM((1, tokens), jnp.int32),
            pltpu.VMEM((8, 2, 2, few, features), bf16),
            pltpu.VMEM((8, 2, few, features), bf16),
            pltpu.VMEM((8, 2, few, features), bf16),
            pltpu.VMEM((2, 3, 2, few, features), bf16),
            pltpu.VMEM((2, 2, few, features), bf16),
            pltpu.VMEM((3, few, features), bf16),
            dma((4,)), dma((28,)), dma((8, 4)), dma((8, 2)), dma((8, 2)), dma((8, 2)), dma((2, 3, 2)),
            dma((2, 2)), dma((3,)), dma((3,)), dma((3,)), dma((3,)), dma((3,)), dma((4,)), dma((4,)),
        ],
        compiler_params=pltpu.CompilerParams(
            collective_id=0, has_side_effects=True, vmem_limit_bytes=48 * 1024 * 1024
        ),
        name="exchange",
    )(*held, round_seed)
    total, input_rows = (pltpu.with_memory_space_constraint(v, pltpu.VMEM) for v in (total, input_rows))
    return pl.pallas_call(
        store_kernel,
        out_shape=(jax.ShapeDtypeStruct((features, ff), f32), jax.ShapeDtypeStruct((few, features), bf16)),
        in_specs=[vmem, vmem],
        out_specs=(hbm, hbm),
        scratch_shapes=[dma((9,))],
        compiler_params=pltpu.CompilerParams(vmem_limit_bytes=4 * 1024 * 1024),
        name="store",
    )(total, input_rows)


def solution(mesh):
    placed = (P("col", "row"), P("row", "col"), P("row", "col"), P(), P("row"))
    return jax.shard_map(
        shards,
        mesh=mesh,
        in_specs=placed,
        out_specs=(P("row", "col"), P("col", "row")),
        check_vma=False,
    )
```

```python
import jax
import jax.numpy as jnp
from jax import lax
from jax.experimental import pallas as pl
from jax.experimental.pallas import tpu as pltpu
from jax.sharding import PartitionSpec as P

MESH = pl.DeviceIdType.MESH
NX, NY, NH = 4, 4, 4
OWN, LEFT, RIGHT, FAR, OWN2, LEFT2, RIGHT2, FAR2 = range(8)
SHARDS = ((0, 0), (3, 0), (1, 0), (2, 0), (0, 1), (3, 1), (1, 1), (2, 1))


def device(x, lo, y, hi, core):
    return (x * 2 + lo, (y * NH + hi) * 2 + core)


def exchange_kernel(
    act_hbm, weight_hbm, grad_hbm, base_hbm, seed_ref, total_ref, out_ref,
    g_ref, a_ref, grad, weight, turned, turned_act, base_row, part, crecv, ssum, yrecv, tsum, zrecv,
    lsem, gs, gr, cs, cr, ys, yr, zs, zr, azs, azr, ays, ayr, acs, acr,
):
    row, col = lax.axis_index("row"), lax.axis_index("col")
    x, lo = lax.div(row, 2), lax.rem(row, 2)
    y, hi, core = lax.div(col, 8), lax.rem(lax.div(col, 2), 4), lax.rem(col, 2)
    tokens, ff = grad.shape
    features = weight.shape[0]
    block = tokens // 4
    here = device(x, lo, y, hi, core)
    right = device(lax.rem(x + 1, NX), lo, y, hi, core)
    left = device(lax.rem(x + 3, NX), lo, y, hi, core)
    pair = device(x, 1 - lo, y, hi, core)
    sibling = device(x, lo, y, hi, 1 - core)

    def at_y(yy):
        return device(x, lo, yy, hi, core)

    def at_hi(hh):
        return device(x, lo, y, hh, core)

    def lo_of(i):
        return lax.rem(lo + SHARDS[i][1], 2)

    def root(i):
        return lax.rem(x + SHARDS[i][0], NX)


    def remote(src, dst, send, recv, to):
        return pltpu.make_async_remote_copy(
            src_ref=src, dst_ref=dst, send_sem=send, recv_sem=recv, device_id=to, device_id_type=MESH
        )

    loads = [
        pltpu.make_async_copy(base_hbm, base_row, lsem.at[0]),
        pltpu.make_async_copy(grad_hbm, grad, lsem.at[1]),
        pltpu.make_async_copy(act_hbm, a_ref.at[y, hi, core], lsem.at[2]),
        pltpu.make_async_copy(weight_hbm, weight, lsem.at[3]),
    ]
    for load in loads:
        load.start()

    barrier = pltpu.get_barrier_semaphore()
    peers = [right, left, pair, sibling]
    peers += [at_y(lax.rem(y + d, NY)) for d in (1, 2, 3)]
    peers += [at_hi(lax.rem(hi + d, NH)) for d in (1, 2, 3)]
    for peer in peers:
        pl.semaphore_signal(barrier, inc=1, device_id=peer, device_id_type=MESH)

    for load in loads[:3]:
        load.wait()
    base = jnp.transpose(jnp.broadcast_to(base_row[...], (tokens, tokens)))
    mixed_seed = seed_ref[0] * jnp.int32(1013904223)
    first = col * ff

    def round_rows(half):
        rows = slice(half * 2 * block, (half + 1) * 2 * block)

        def round_columns(n, _):
            columns = pl.ds(pl.multiple_of(n * 128, 128), 128)
            counter = base[rows] + (first + n * 128 + lax.broadcasted_iota(jnp.int32, (2 * block, 128), 1))
            mixed = counter * jnp.int32(747796405) + mixed_seed
            mixed = mixed ^ (mixed >> 15)
            mixed = mixed * jnp.int32(277803737)
            mixed = mixed ^ (mixed >> 16)
            level = (mixed & 255).astype(jnp.float32)
            scaled = grad[rows, columns].astype(jnp.float32) * 4.0 + (level + 0.5) / 256.0
            rounded = (jnp.floor(scaled) / 4.0).astype(jnp.bfloat16)
            g_ref[x, lo, pl.ds(2 * half, 2), :, columns] = rounded.reshape(2, block, 128)
            return 0

        lax.fori_loop(0, ff // 128, round_columns, 0)

    round_rows(0)
    pl.semaphore_wait(barrier, len(peers))

    sends = []

    def send_g(i, j, to):
        where = g_ref.at[root(i), lo_of(i), j]
        copy = remote(where, where, gs.at[len(sends)], gr.at[root(i), lo_of(i), j], to)
        copy.start()
        sends.append(copy)

    def wait_g(i, *js):
        for j in js:
            where = g_ref.at[root(i), lo_of(i), j]
            remote(where, where, gs.at[0], gr.at[root(i), lo_of(i), j], here).wait_recv()

    def core_copy(i, q):
        return remote(part.at[i, q, 1 - core], crecv.at[i, q], cs.at[i, q], cr.at[i, q], sibling)

    def project(*units):
        rows = 2 * block

        left_side = jnp.concatenate(
            [g_ref[root(i), lo_of(i), pl.ds(2 * q, 2)].reshape(rows, ff) for i, q in units], axis=0
        )
        value = lax.dot_general(
            left_side, turned[...], (((1,), (0,)), ((), ())), preferred_element_type=jnp.float32
        ).astype(jnp.bfloat16)
        for u, (i, q) in enumerate(units):
            part[i, q] = value[u * rows : (u + 1) * rows].reshape(2, block, features)
        for i, q in units:
            core_copy(i, q).start()

    def y_copy(i, q):
        k = lax.rem(y + NY - root(i), NY) - 1
        return remote(ssum.at[i, q], yrecv.at[lo_of(i), k, q], ys.at[i, q], yr.at[lo_of(i), k, q], at_y(root(i)))

    def add_cores(*units):
        for i, q in units:
            core_copy(i, q).wait_recv()
            ssum[i, q] = (part[i, q, core].astype(jnp.float32) + crecv[i, q].astype(jnp.float32)).astype(jnp.bfloat16)

            @pl.when(y != root(i))
            def _():
                y_copy(i, q).start()

    def z_copy(lo_root, q):
        to = 2 * lo_root + q
        k = lax.rem(hi + NH - to, NH) - 1
        return remote(tsum.at[lo_root, q], zrecv.at[k], zs.at[lo_root, q], zr.at[k], at_hi(to))

    def add_columns(*units):
        for i, q in units:

            @pl.when(y == root(i))
            def _():
                lo_root = lo_of(i)
                total = ssum[i, q].astype(jnp.float32)
                for k in range(3):
                    where = yrecv.at[lo_root, k, q]
                    remote(where, where, ys.at[i, q], yr.at[lo_root, k, q], here).wait_recv()
                    total += yrecv[lo_root, k, q].astype(jnp.float32)
                tsum[lo_root, q] = total.astype(jnp.bfloat16)

                @pl.when(hi != 2 * lo_root + q)
                def _():
                    z_copy(lo_root, q).start()

    def az_copy(d):
        where = a_ref.at[y, hi, core]
        return remote(where, where, azs.at[d - 1], azr.at[d - 1], at_hi(lax.rem(hi + d, NH)))

    def az_wait(d):
        where = a_ref.at[y, lax.rem(hi + NH - d, NH), core]
        remote(where, where, azs.at[d - 1], azr.at[d - 1], here).wait_recv()

    def ay_copy(n):
        up, down = lax.rem(y + 1, NY), lax.rem(y + NY - 1, NY)
        owner, half, to, k = ((y, 0, up, 0), (y, 1, down, 2), (y, 1, up, 0), (y, 0, down, 2), (down, 0, up, 1), (up, 1, down, 1))[n]
        where = a_ref.at[owner, pl.ds(2 * half, 2), core]
        return remote(where, where, ays.at[n], ayr.at[k, half], at_y(to))

    def ay_wait(d, half):
        where = a_ref.at[lax.rem(y + NY - d, NY), pl.ds(2 * half, 2), core]
        remote(where, where, ays.at[0], ayr.at[d - 1, half], here).wait_recv()

    def ac_copy(d):
        where = a_ref.at[lax.rem(y + NY - d, NY), :, core]
        return remote(where, where, acs.at[d], acr.at[d], sibling)

    def ac_wait(d):
        where = a_ref.at[lax.rem(y + NY - d, NY), :, 1 - core]
        remote(where, where, acs.at[d], acr.at[d], here).wait_recv()

    def turn_act(plane):
        for r in range(NX):
            rows = a_ref[r, pl.ds(2 * plane, 2)].reshape(tokens, features)
            turned_act[:, r * tokens : (r + 1) * tokens] = jnp.transpose(rows)

    def accumulate(plane, span, last):
        lowest, highest = span
        value = lax.dot_general(
            turned_act[...],
            g_ref[:, plane, :, :, lowest:highest].reshape(NX * tokens, highest - lowest),
            (((1,), (0,)), ((), ())),
            preferred_element_type=jnp.float32,
        )
        if last:
            value = (total_ref[:, lowest:highest] + value) * (NX * 2 * tokens) ** (-0.5)
        total_ref[:, lowest:highest] = value

    spans = [(n, min(n + 512, ff)) for n in range(0, ff, 512)]

    for d in (1, 2, 3):
        az_copy(d).start()
    send_g(OWN, 0, right)
    send_g(OWN, 1, left)
    send_g(OWN, 0, pair)
    send_g(OWN, 1, pair)
    round_rows(1)
    for j, k in ((2, 3), (1, 0), (3, 2)):
        send_g(OWN, j, right)
        send_g(OWN, k, left)
    send_g(OWN, 2, pair)
    send_g(OWN, 3, pair)
    loads[3].wait()

    def turn_weight(n, _):
        some = pl.ds(pl.multiple_of(n * 128, 128), 128)
        turned[:, some] = jnp.transpose(weight[some, :])
        return 0

    lax.fori_loop(0, features // 128, turn_weight, 0)
    project((OWN, 0), (OWN, 1))
    wait_g(LEFT, 0)
    send_g(LEFT, 0, right)
    wait_g(RIGHT, 1)
    send_g(RIGHT, 1, left)
    add_cores((OWN, 0), (OWN, 1))
    wait_g(LEFT, 2)
    send_g(LEFT, 2, right)
    wait_g(RIGHT, 3)
    send_g(RIGHT, 3, left)
    for d in (1, 2, 3):
        az_wait(d)
    for n in range(4):
        ay_copy(n).start()
    ac_copy(0).start()
    wait_g(OWN2, 0)
    send_g(OWN2, 0, right)
    send_g(OWN2, 0, left)
    wait_g(LEFT, 1, 3)
    wait_g(RIGHT, 0, 2)
    project((LEFT, 0), (LEFT, 1), (RIGHT, 0), (RIGHT, 1))
    wait_g(OWN2, 1)
    send_g(OWN2, 1, right)
    send_g(OWN2, 1, left)
    wait_g(FAR, 0, 1)
    send_g(FAR, 0, pair)
    send_g(FAR, 1, pair)
    ay_wait(1, 0)
    ay_copy(4).start()
    ay_wait(3, 1)
    ay_copy(5).start()
    wait_g(OWN2, 2)
    send_g(OWN2, 2, right)
    send_g(OWN2, 2, left)
    add_cores((LEFT, 0), (LEFT, 1), (RIGHT, 0), (RIGHT, 1))
    wait_g(FAR, 2, 3)
    send_g(FAR, 2, pair)
    send_g(FAR, 3, pair)
    wait_g(OWN2, 3)
    send_g(OWN2, 3, right)
    send_g(OWN2, 3, left)
    project((OWN2, 0), (OWN2, 1), (FAR, 0), (FAR, 1))
    add_columns((OWN, 0), (OWN, 1))
    add_cores((OWN2, 0), (OWN2, 1), (FAR, 0), (FAR, 1))
    wait_g(LEFT2, 0, 1)
    wait_g(RIGHT2, 0, 1)
    wait_g(FAR2, 0, 1)
    project((LEFT2, 0), (RIGHT2, 0), (FAR2, 0))
    ay_wait(1, 1)
    ac_copy(1).start()
    ay_wait(3, 0)
    ac_copy(3).start()
    ay_wait(2, 0)
    ay_wait(2, 1)
    ac_copy(2).start()
    add_cores((LEFT2, 0), (RIGHT2, 0), (FAR2, 0))
    for d in range(4):
        ac_wait(d)
    turn_act(lo)
    for span in spans[:2]:
        accumulate(lo, span, False)
    wait_g(LEFT2, 2, 3)
    wait_g(RIGHT2, 2, 3)
    wait_g(FAR2, 2, 3)
    project((LEFT2, 1), (RIGHT2, 1), (FAR2, 1))
    add_columns((LEFT, 0), (LEFT, 1), (RIGHT, 0), (RIGHT, 1))
    add_cores((LEFT2, 1), (RIGHT2, 1), (FAR2, 1))
    add_columns((OWN2, 0), (OWN2, 1), (FAR, 0), (FAR, 1))
    for span in spans[2:]:
        accumulate(lo, span, False)
    turn_act(1 - lo)
    add_columns((LEFT2, 0), (RIGHT2, 0), (FAR2, 0))
    for span in spans[:3]:
        accumulate(1 - lo, span, True)
    add_columns((LEFT2, 1), (RIGHT2, 1), (FAR2, 1))
    for span in spans[3:]:
        accumulate(1 - lo, span, True)

    total = tsum[lax.div(hi, 2), lax.rem(hi, 2)].astype(jnp.float32)
    for k in range(3):
        remote(zrecv.at[k], zrecv.at[k], zs.at[0, 0], zr.at[k], here).wait_recv()
        total += zrecv[k].astype(jnp.float32)
    out_ref[...] = total.astype(jnp.bfloat16)

    for copy in sends:
        copy.wait_send()
    for i in range(8):
        for q in range(2):
            core_copy(i, q).wait_send()

            @pl.when(y != root(i))
            def _():
                y_copy(i, q).wait_send()

            @pl.when((y == root(i)) & (hi != 2 * lo_of(i) + q))
            def _():
                z_copy(lo_of(i), q).wait_send()

    for d in (1, 2, 3):
        az_copy(d).wait_send()
    for n in range(6):
        ay_copy(n).wait_send()
    for d in range(4):
        ac_copy(d).wait_send()


def store_kernel(total_ref, rows_ref, total_hbm, rows_hbm, sem):
    pieces = 8
    step = total_ref.shape[0] // pieces
    copies = [pltpu.make_async_copy(rows_ref, rows_hbm, sem.at[pieces])]
    for n in range(pieces):
        some = pl.ds(n * step, step)
        copies.append(pltpu.make_async_copy(total_ref.at[some], total_hbm.at[some], sem.at[n]))
    for copy in copies:
        copy.start()
    for copy in copies:
        copy.wait()


def shards(activations, up_weight, out_grad, round_seed, counter_base):
    tokens, ff = out_grad.shape
    few, features = activations.shape
    bf16, f32, dma = jnp.bfloat16, jnp.float32, pltpu.SemaphoreType.DMA
    vmem, hbm = pl.BlockSpec(memory_space=pltpu.VMEM), pl.BlockSpec(memory_space=pltpu.HBM)
    operands = (activations, up_weight, out_grad, counter_base.reshape(1, tokens))
    held = [pltpu.with_memory_space_constraint(v, pltpu.HBM) for v in operands]
    total, input_rows = pl.pallas_call(
        exchange_kernel,
        out_shape=(pltpu.VMEM((features, ff), f32), pltpu.VMEM((few, features), bf16)),
        in_specs=[hbm] * 4 + [pl.BlockSpec(memory_space=pltpu.SMEM)],
        out_specs=(vmem, vmem),
        scratch_shapes=[
            pltpu.VMEM((NX, 2, 4, tokens // 4, ff), bf16),
            pltpu.VMEM((NY, NH, 2, few, features), bf16),
            pltpu.VMEM((tokens, ff), bf16),
            pltpu.VMEM((features, ff), bf16),
            pltpu.VMEM((ff, features), bf16),
            pltpu.VMEM((features, NX * tokens), bf16),
            pltpu.VMEM((1, tokens), jnp.int32),
            pltpu.VMEM((8, 2, 2, few, features), bf16),
            pltpu.VMEM((8, 2, few, features), bf16),
            pltpu.VMEM((8, 2, few, features), bf16),
            pltpu.VMEM((2, 3, 2, few, features), bf16),
            pltpu.VMEM((2, 2, few, features), bf16),
            pltpu.VMEM((3, few, features), bf16),
            dma((4,)), dma((28,)), dma((NX, 2, 4)), dma((8, 2)), dma((8, 2)), dma((8, 2)), dma((2, 3, 2)),
            dma((2, 2)), dma((3,)), dma((3,)), dma((3,)), dma((6,)), dma((3, 2)), dma((4,)), dma((4,)),
        ],
        compiler_params=pltpu.CompilerParams(
            collective_id=0, has_side_effects=True, vmem_limit_bytes=48 * 1024 * 1024
        ),
        name="exchange",
    )(*held, round_seed)
    total, input_rows = (pltpu.with_memory_space_constraint(v, pltpu.VMEM) for v in (total, input_rows))
    return pl.pallas_call(
        store_kernel,
        out_shape=(jax.ShapeDtypeStruct((features, ff), f32), jax.ShapeDtypeStruct((few, features), bf16)),
        in_specs=[vmem, vmem],
        out_specs=(hbm, hbm),
        scratch_shapes=[dma((9,))],
        compiler_params=pltpu.CompilerParams(vmem_limit_bytes=4 * 1024 * 1024),
        name="store",
    )(total, input_rows)


def solution(mesh):
    placed = (P("col", "row"), P("row", "col"), P("row", "col"), P(), P("row"))
    return jax.shard_map(
        shards,
        mesh=mesh,
        in_specs=placed,
        out_specs=(P("row", "col"), P("col", "row")),
        check_vma=False,
    )
```

```python
import jax
import jax.numpy as jnp
from jax import lax
from jax.experimental import pallas as pl
from jax.experimental.pallas import tpu as pltpu
from jax.sharding import PartitionSpec as P

MESH = pl.DeviceIdType.MESH
NX, NY, NH = 4, 4, 4
OWN, LEFT, RIGHT, FAR, OWN2, LEFT2, RIGHT2, FAR2 = range(8)
SHARDS = ((0, 0), (3, 0), (1, 0), (2, 0), (0, 1), (3, 1), (1, 1), (2, 1))


def device(x, lo, y, hi, core):
    return (x * 2 + lo, (y * NH + hi) * 2 + core)


def exchange_kernel(
    act_hbm, weight_hbm, grad_hbm, base_hbm, seed_ref, total_ref, out_ref,
    g_ref, a_ref, grad, weight, turned, turned_act, base_row, part, crecv, ssum, yrecv, tsum, zrecv, zpair, zfar,
    lsem, gs, gr, hr, cs, cr, ys, yr, zs, zr, ts, tr, azs, azr, ays, ayr, acs, acr,
):
    row, col = lax.axis_index("row"), lax.axis_index("col")
    x, lo = lax.div(row, 2), lax.rem(row, 2)
    y, hi, core = lax.div(col, 8), lax.rem(lax.div(col, 2), 4), lax.rem(col, 2)
    tokens, ff = grad.shape
    features = weight.shape[0]
    block = tokens // 4
    here = device(x, lo, y, hi, core)
    right = device(lax.rem(x + 1, NX), lo, y, hi, core)
    left = device(lax.rem(x + 3, NX), lo, y, hi, core)
    pair = device(x, 1 - lo, y, hi, core)
    sibling = device(x, lo, y, hi, 1 - core)

    def at_y(yy):
        return device(x, lo, yy, hi, core)

    def at_hi(hh):
        return device(x, lo, y, hh, core)

    def lo_of(i):
        return lax.rem(lo + SHARDS[i][1], 2)

    def root(i):
        return lax.rem(x + SHARDS[i][0], NX)


    def remote(src, dst, send, recv, to):
        return pltpu.make_async_remote_copy(
            src_ref=src, dst_ref=dst, send_sem=send, recv_sem=recv, device_id=to, device_id_type=MESH
        )

    loads = [
        pltpu.make_async_copy(base_hbm, base_row, lsem.at[0]),
        pltpu.make_async_copy(grad_hbm, grad, lsem.at[1]),
        pltpu.make_async_copy(act_hbm, a_ref.at[y, hi, core], lsem.at[2]),
        pltpu.make_async_copy(weight_hbm, weight, lsem.at[3]),
    ]
    for load in loads[:3]:
        load.start()

    barrier = pltpu.get_barrier_semaphore()
    peers = [right, left, pair, sibling]
    peers += [at_y(lax.rem(y + d, NY)) for d in (1, 2, 3)]
    peers += [at_hi(lax.rem(hi + d, NH)) for d in (1, 2, 3)]
    for peer in peers:
        pl.semaphore_signal(barrier, inc=1, device_id=peer, device_id_type=MESH)

    for load in loads[:3]:
        load.wait()
    loads[3].start()
    base = jnp.transpose(jnp.broadcast_to(base_row[...], (tokens, tokens)))
    mixed_seed = seed_ref[0] * jnp.int32(1013904223)
    first = col * ff

    def round_rows(j, count):
        rows = slice(j * block, (j + count) * block)

        def round_columns(n, _):
            columns = pl.ds(pl.multiple_of(n * 128, 128), 128)
            counter = base[rows] + (first + n * 128 + lax.broadcasted_iota(jnp.int32, (count * block, 128), 1))
            mixed = counter * jnp.int32(747796405) + mixed_seed
            mixed = mixed ^ (mixed >> 15)
            mixed = mixed * jnp.int32(277803737)
            mixed = mixed ^ (mixed >> 16)
            level = (mixed & 255).astype(jnp.float32)
            scaled = grad[rows, columns].astype(jnp.float32) * 4.0 + (level + 0.5) / 256.0
            rounded = (jnp.floor(scaled) / 4.0).astype(jnp.bfloat16)
            g_ref[x, lo, pl.ds(j, count), :, columns] = rounded.reshape(count, block, 128)
            return 0

        lax.fori_loop(0, ff // 128, round_columns, 0)

    round_rows(0, 1)
    pl.semaphore_wait(barrier, len(peers))

    sends = []

    def send_g(i, j, to):
        where = g_ref.at[root(i), lo_of(i), j]
        copy = remote(where, where, gs.at[len(sends)], gr.at[root(i), lo_of(i), j], to)
        copy.start()
        sends.append(copy)

    def wait_g(i, *js):
        for j in js:
            where = g_ref.at[root(i), lo_of(i), j]
            remote(where, where, gs.at[0], gr.at[root(i), lo_of(i), j], here).wait_recv()

    def half_chunk(i, half):
        return g_ref.at[root(i), lo_of(i), 3, pl.ds(half * (block // 2), block // 2)]

    def send_half(i, half, to):
        copy = remote(half_chunk(i, half), half_chunk(i, half), gs.at[len(sends)], hr.at[half], to)
        copy.start()
        sends.append(copy)

    def wait_half(half):
        where = half_chunk(FAR2, half)
        remote(where, where, gs.at[0], hr.at[half], here).wait_recv()

    def core_copy(i, q):
        return remote(part.at[i, q, 1 - core], crecv.at[i, q], cs.at[i, q], cr.at[i, q], sibling)

    def project(*pieces):
        left_side = jnp.concatenate(
            [g_ref[root(i), lo_of(i), pl.ds(j, n)].reshape(n * block, ff) for i, j, n in pieces], axis=0
        )
        value = lax.dot_general(
            left_side, turned[...], (((1,), (0,)), ((), ())), preferred_element_type=jnp.float32
        ).astype(jnp.bfloat16)
        row = 0
        for i, j, n in pieces:
            for k in range(j, j + n):
                part[i, k // 2, k % 2] = value[row : row + block]
                row += block

    def send_core(*units):
        for i, q in units:
            core_copy(i, q).start()

    def y_copy(i, q):
        k = lax.rem(y + NY - root(i), NY) - 1
        return remote(ssum.at[i, q], yrecv.at[lo_of(i), k, q], ys.at[i, q], yr.at[lo_of(i), k, q], at_y(root(i)))

    def add_cores(*units):
        for i, q in units:
            core_copy(i, q).wait_recv()
            ssum[i, q] = (part[i, q, core].astype(jnp.float32) + crecv[i, q].astype(jnp.float32)).astype(jnp.bfloat16)

            @pl.when(y != root(i))
            def _():
                y_copy(i, q).start()

    def z_copy(q):
        to = 2 * (1 - lo) + q
        k = lax.rem(hi + NH - to, NH) - 1
        return remote(tsum.at[1 - lo, q], zrecv.at[k], zs.at[q], zr.at[k], at_hi(to))

    def sum_columns(i, q):
        lo_root = lo_of(i)
        total = ssum[i, q].astype(jnp.float32)
        for k in range(3):
            where = yrecv.at[lo_root, k, q]
            remote(where, where, ys.at[i, q], yr.at[lo_root, k, q], here).wait_recv()
            total += yrecv[lo_root, k, q].astype(jnp.float32)
        tsum[lo_root, q] = total.astype(jnp.bfloat16)

    def add_columns(*units):
        for i, q in units:

            @pl.when(y == root(i))
            def _():
                sum_columns(i, q)

                @pl.when(hi != 2 * (1 - lo) + q)
                def _():
                    z_copy(q).start()

    parity = lax.rem(hi, 2)
    far = lax.rem(lax.div(hi, 2) + lo, 2)
    keep = lax.rem(parity + far, 2)

    def pair_copy():
        return remote(tsum.at[lo, 1 - keep], zpair, ts.at[0], tr.at[0], at_hi(hi + 1 - 2 * parity))

    def far_copy():
        return remote(tsum.at[lo, keep], zfar, ts.at[1], tr.at[1], at_hi(lax.rem(hi + 3 - 2 * parity, NH)))

    def add_plane(*shards):
        for i in shards:

            @pl.when(y == root(i))
            def _():
                for q in range(2):
                    sum_columns(i, q)
                pair_copy().start()

    def pass_on():
        remote(zpair, zpair, ts.at[0], tr.at[0], here).wait_recv()

        @pl.when(far == 1)
        def _():
            tsum[lo, keep] = (tsum[lo, keep].astype(jnp.float32) + zpair[...].astype(jnp.float32)).astype(jnp.bfloat16)
            far_copy().start()

    def az_copy(d):
        where = a_ref.at[y, hi, core]
        return remote(where, where, azs.at[d - 1], azr.at[d - 1], at_hi(lax.rem(hi + d, NH)))

    def az_wait(d):
        where = a_ref.at[y, lax.rem(hi + NH - d, NH), core]
        remote(where, where, azs.at[d - 1], azr.at[d - 1], here).wait_recv()

    def ay_copy(n):
        up, down = lax.rem(y + 1, NY), lax.rem(y + NY - 1, NY)
        owner, half, to, k = ((y, 0, up, 0), (y, 1, down, 2), (y, 1, up, 0), (y, 0, down, 2), (down, 0, up, 1), (up, 1, down, 1))[n]
        where = a_ref.at[owner, pl.ds(2 * half, 2), core]
        return remote(where, where, ays.at[n], ayr.at[k, half], at_y(to))

    def ay_wait(d, half):
        where = a_ref.at[lax.rem(y + NY - d, NY), pl.ds(2 * half, 2), core]
        remote(where, where, ays.at[0], ayr.at[d - 1, half], here).wait_recv()

    def ac_copy(d):
        where = a_ref.at[lax.rem(y + NY - d, NY), :, core]
        return remote(where, where, acs.at[d], acr.at[d], sibling)

    def ac_wait(d):
        where = a_ref.at[lax.rem(y + NY - d, NY), :, 1 - core]
        remote(where, where, acs.at[d], acr.at[d], here).wait_recv()

    def turn_act(plane):
        for r in range(NX):
            rows = a_ref[r, pl.ds(2 * plane, 2)].reshape(tokens, features)
            turned_act[:, r * tokens : (r + 1) * tokens] = jnp.transpose(rows)

    def accumulate(plane, span, last):
        lowest, highest = span
        value = lax.dot_general(
            turned_act[...],
            g_ref[:, plane, :, :, lowest:highest].reshape(NX * tokens, highest - lowest),
            (((1,), (0,)), ((), ())),
            preferred_element_type=jnp.float32,
        )
        if last:
            value = (total_ref[:, lowest:highest] + value) * (NX * 2 * tokens) ** (-0.5)
        total_ref[:, lowest:highest] = value

    spans = [(n, min(n + 512, ff)) for n in range(0, ff, 512)]

    for d in (1, 2, 3):
        az_copy(d).start()
    send_g(OWN, 0, right)
    round_rows(1, 1)
    send_g(OWN, 1, left)
    round_rows(2, 2)
    send_g(OWN, 3, pair)
    send_g(OWN, 0, pair)
    for j, k in ((2, 3), (1, 0), (3, 2)):
        send_g(OWN, j, right)
        send_g(OWN, k, left)
    send_g(OWN, 1, pair)
    send_g(OWN, 2, pair)
    loads[3].wait()

    def turn_weight(n, _):
        some = pl.ds(pl.multiple_of(n * 128, 128), 128)
        turned[:, some] = jnp.transpose(weight[some, :])
        return 0

    lax.fori_loop(0, features // 128, turn_weight, 0)
    project((OWN, 0, 4))
    send_core((OWN, 0), (OWN, 1))
    wait_g(LEFT, 0)
    send_g(LEFT, 0, right)
    wait_g(RIGHT, 1)
    send_g(RIGHT, 1, left)
    add_cores((OWN, 0), (OWN, 1))
    wait_g(LEFT, 2)
    send_g(LEFT, 2, right)
    wait_g(RIGHT, 3)
    send_g(RIGHT, 3, left)
    for d in (1, 2, 3):
        az_wait(d)
    for n in range(4):
        ay_copy(n).start()
    ac_copy(0).start()
    wait_g(OWN2, 3)
    send_g(OWN2, 3, right)
    send_g(OWN2, 3, left)
    wait_g(LEFT, 1, 3)
    wait_g(RIGHT, 0, 2)
    project((LEFT, 0, 4), (RIGHT, 0, 4))
    send_core((LEFT, 0), (LEFT, 1), (RIGHT, 0), (RIGHT, 1))
    wait_g(OWN2, 0)
    send_g(OWN2, 0, right)
    send_g(OWN2, 0, left)
    wait_g(FAR, 0, 1)
    send_g(FAR, 0, pair)
    send_g(FAR, 1, pair)
    ay_wait(1, 0)
    ay_copy(4).start()
    ay_wait(3, 1)
    ay_copy(5).start()
    wait_g(OWN2, 1)
    send_g(OWN2, 1, right)
    send_g(OWN2, 1, left)
    add_cores((LEFT, 0), (LEFT, 1), (RIGHT, 0), (RIGHT, 1))
    wait_g(FAR, 2, 3)
    send_g(FAR, 2, pair)
    wait_g(OWN2, 2)
    project((FAR, 0, 4), (OWN2, 0, 4))
    send_core((FAR, 0), (FAR, 1), (OWN2, 0), (OWN2, 1))
    wait_g(LEFT2, 3)
    send_half(LEFT2, 0, right)
    send_g(OWN2, 2, right)
    wait_g(RIGHT2, 3)
    send_half(RIGHT2, 1, left)
    send_g(OWN2, 2, left)
    add_plane(OWN)
    ay_wait(1, 1)
    ac_copy(1).start()
    ay_wait(3, 0)
    ac_copy(3).start()
    add_cores((FAR, 0), (FAR, 1), (OWN2, 0), (OWN2, 1))
    wait_g(LEFT2, 0)
    wait_g(RIGHT2, 0)
    wait_g(FAR2, 0)
    project((LEFT2, 3, 1), (RIGHT2, 3, 1), (LEFT2, 0, 1), (RIGHT2, 0, 1), (FAR2, 0, 1))

    @pl.when(core == 0)
    def _():
        send_core((LEFT2, 1), (RIGHT2, 1))

    @pl.when(core == 1)
    def _():
        send_core((FAR2, 0), (LEFT2, 0), (RIGHT2, 0))

    ay_wait(2, 0)
    ay_wait(2, 1)
    ac_copy(2).start()
    wait_g(LEFT2, 1)
    wait_g(RIGHT2, 1)
    wait_g(FAR2, 1)
    project((LEFT2, 1, 1), (RIGHT2, 1, 1), (FAR2, 1, 1))

    @pl.when(core == 0)
    def _():
        send_core((FAR2, 0), (LEFT2, 0), (RIGHT2, 0))
        add_cores((FAR2, 0), (LEFT2, 0), (RIGHT2, 0))

    @pl.when(core == 1)
    def _():
        add_cores((LEFT2, 1), (RIGHT2, 1))

    wait_half(0)
    wait_half(1)
    project((FAR2, 3, 1))

    @pl.when(core == 0)
    def _():
        send_core((FAR2, 1))

    wait_g(LEFT2, 2)
    wait_g(RIGHT2, 2)
    wait_g(FAR2, 2)
    project((LEFT2, 2, 1), (RIGHT2, 2, 1), (FAR2, 2, 1))

    @pl.when(core == 1)
    def _():
        send_core((FAR2, 1), (LEFT2, 1), (RIGHT2, 1))
        add_cores((FAR2, 0), (LEFT2, 0), (RIGHT2, 0), (FAR2, 1))

    add_plane(FAR, LEFT, RIGHT)
    add_columns((OWN2, 0), (OWN2, 1))
    for d in range(4):
        ac_wait(d)
    turn_act(lo)

    @pl.when(core == 0)
    def _():
        add_cores((FAR2, 1), (LEFT2, 1), (RIGHT2, 1))

    @pl.when(core == 1)
    def _():
        add_columns((LEFT2, 1), (RIGHT2, 1))

    accumulate(lo, spans[0], False)
    accumulate(lo, spans[1], False)
    add_columns((FAR2, 0), (LEFT2, 0), (RIGHT2, 0))
    pass_on()
    for span in spans[2:]:
        accumulate(lo, span, False)
    turn_act(1 - lo)

    @pl.when(core == 0)
    def _():
        add_columns((FAR2, 1), (LEFT2, 1), (RIGHT2, 1))

    @pl.when(core == 1)
    def _():
        add_columns((FAR2, 1))

    for span in spans:
        accumulate(1 - lo, span, True)

    total = tsum[lax.div(hi, 2), parity].astype(jnp.float32)

    @pl.when(far == 0)
    def _():
        remote(zfar, zfar, ts.at[1], tr.at[1], here).wait_recv()
        out_ref[...] = (total + zpair[...].astype(jnp.float32) + zfar[...].astype(jnp.float32)).astype(jnp.bfloat16)

    @pl.when(far == 1)
    def _():
        for k in range(3):
            remote(zrecv.at[k], zrecv.at[k], zs.at[0], zr.at[k], here).wait_recv()
        rest = sum(zrecv[k].astype(jnp.float32) for k in range(3))
        out_ref[...] = (total + rest).astype(jnp.bfloat16)

    for copy in sends:
        copy.wait_send()
    for i in range(8):
        for q in range(2):
            core_copy(i, q).wait_send()

            @pl.when(y != root(i))
            def _():
                y_copy(i, q).wait_send()

    for q in range(2):

        @pl.when(hi != 2 * (1 - lo) + q)
        def _():
            z_copy(q).wait_send()

    pair_copy().wait_send()

    @pl.when(far == 1)
    def _():
        far_copy().wait_send()

    for d in (1, 2, 3):
        az_copy(d).wait_send()
    for n in range(6):
        ay_copy(n).wait_send()
    for d in range(4):
        ac_copy(d).wait_send()


def store_kernel(total_ref, rows_ref, total_hbm, rows_hbm, sem):
    pieces = 8
    step = total_ref.shape[0] // pieces
    copies = [pltpu.make_async_copy(rows_ref, rows_hbm, sem.at[pieces])]
    for n in range(pieces):
        some = pl.ds(n * step, step)
        copies.append(pltpu.make_async_copy(total_ref.at[some], total_hbm.at[some], sem.at[n]))
    for copy in copies:
        copy.start()
    for copy in copies:
        copy.wait()


def shards(activations, up_weight, out_grad, round_seed, counter_base):
    tokens, ff = out_grad.shape
    few, features = activations.shape
    bf16, f32, dma = jnp.bfloat16, jnp.float32, pltpu.SemaphoreType.DMA
    vmem, hbm = pl.BlockSpec(memory_space=pltpu.VMEM), pl.BlockSpec(memory_space=pltpu.HBM)
    operands = (activations, up_weight, out_grad, counter_base.reshape(1, tokens))
    held = [pltpu.with_memory_space_constraint(v, pltpu.HBM) for v in operands]
    total, input_rows = pl.pallas_call(
        exchange_kernel,
        out_shape=(pltpu.VMEM((features, ff), f32), pltpu.VMEM((few, features), bf16)),
        in_specs=[hbm] * 4 + [pl.BlockSpec(memory_space=pltpu.SMEM)],
        out_specs=(vmem, vmem),
        scratch_shapes=[
            pltpu.VMEM((NX, 2, 4, tokens // 4, ff), bf16),
            pltpu.VMEM((NY, NH, 2, few, features), bf16),
            pltpu.VMEM((tokens, ff), bf16),
            pltpu.VMEM((features, ff), bf16),
            pltpu.VMEM((ff, features), bf16),
            pltpu.VMEM((features, NX * tokens), bf16),
            pltpu.VMEM((1, tokens), jnp.int32),
            pltpu.VMEM((8, 2, 2, few, features), bf16),
            pltpu.VMEM((8, 2, few, features), bf16),
            pltpu.VMEM((8, 2, few, features), bf16),
            pltpu.VMEM((2, 3, 2, few, features), bf16),
            pltpu.VMEM((2, 2, few, features), bf16),
            pltpu.VMEM((3, few, features), bf16),
            pltpu.VMEM((few, features), bf16),
            pltpu.VMEM((few, features), bf16),
            dma((4,)), dma((29,)), dma((NX, 2, 4)), dma((2,)), dma((8, 2)), dma((8, 2)), dma((8, 2)), dma((2, 3, 2)),
            dma((2,)), dma((3,)), dma((2,)), dma((2,)), dma((3,)), dma((3,)), dma((6,)), dma((3, 2)), dma((4,)), dma((4,)),
        ],
        compiler_params=pltpu.CompilerParams(
            collective_id=0, has_side_effects=True, vmem_limit_bytes=48 * 1024 * 1024
        ),
        name="exchange",
    )(*held, round_seed)
    total, input_rows = (pltpu.with_memory_space_constraint(v, pltpu.VMEM) for v in (total, input_rows))
    return pl.pallas_call(
        store_kernel,
        out_shape=(jax.ShapeDtypeStruct((features, ff), f32), jax.ShapeDtypeStruct((few, features), bf16)),
        in_specs=[vmem, vmem],
        out_specs=(hbm, hbm),
        scratch_shapes=[dma((9,))],
        compiler_params=pltpu.CompilerParams(vmem_limit_bytes=4 * 1024 * 1024),
        name="store",
    )(total, input_rows)


def solution(mesh):
    placed = (P("col", "row"), P("row", "col"), P("row", "col"), P(), P("row"))
    return jax.shard_map(
        shards,
        mesh=mesh,
        in_specs=placed,
        out_specs=(P("row", "col"), P("col", "row")),
        check_vma=False,
    )
```

```python
import jax
import jax.numpy as jnp
from jax import lax
from jax.experimental import pallas as pl
from jax.experimental.pallas import tpu as pltpu
from jax.sharding import PartitionSpec as P

MESH = pl.DeviceIdType.MESH
NX, NY, NH = 4, 4, 4
OWN, LEFT, RIGHT, FAR, OWN2, LEFT2, RIGHT2, FAR2 = range(8)
SHARDS = ((0, 0), (3, 0), (1, 0), (2, 0), (0, 1), (3, 1), (1, 1), (2, 1))


def device(x, lo, y, hi, core):
    return (x * 2 + lo, (y * NH + hi) * 2 + core)


def exchange_kernel(
    act_hbm, weight_hbm, grad_hbm, base_hbm, seed_ref, total_ref, out_ref,
    g_ref, a_ref, grad, weight, turned, turned_act, base_row, part, crecv, ssum, yrecv, tsum, zrecv, zpair, zfar,
    lsem, gs, gr, hr, cs, cr, ys, yr, zs, zr, ts, tr, azs, azr, ays, ayr, acs, acr,
):
    row, col = lax.axis_index("row"), lax.axis_index("col")
    x, lo = lax.div(row, 2), lax.rem(row, 2)
    y, hi, core = lax.div(col, 8), lax.rem(lax.div(col, 2), 4), lax.rem(col, 2)
    tokens, ff = grad.shape
    features = weight.shape[0]
    block = tokens // 4
    here = device(x, lo, y, hi, core)
    right = device(lax.rem(x + 1, NX), lo, y, hi, core)
    left = device(lax.rem(x + 3, NX), lo, y, hi, core)
    pair = device(x, 1 - lo, y, hi, core)
    sibling = device(x, lo, y, hi, 1 - core)

    def at_y(yy):
        return device(x, lo, yy, hi, core)

    def at_hi(hh):
        return device(x, lo, y, hh, core)

    def lo_of(i):
        return lax.rem(lo + SHARDS[i][1], 2)

    def root(i):
        return lax.rem(x + SHARDS[i][0], NX)


    def remote(src, dst, send, recv, to):
        return pltpu.make_async_remote_copy(
            src_ref=src, dst_ref=dst, send_sem=send, recv_sem=recv, device_id=to, device_id_type=MESH
        )

    loads = [
        pltpu.make_async_copy(base_hbm, base_row, lsem.at[0]),
        pltpu.make_async_copy(grad_hbm, grad, lsem.at[1]),
        pltpu.make_async_copy(act_hbm, a_ref.at[y, hi, core], lsem.at[2]),
        pltpu.make_async_copy(weight_hbm, weight, lsem.at[3]),
    ]
    for load in loads[:3]:
        load.start()

    barrier = pltpu.get_barrier_semaphore()
    peers = [right, left, pair, sibling]
    peers += [at_y(lax.rem(y + d, NY)) for d in (1, 2, 3)]
    peers += [at_hi(lax.rem(hi + d, NH)) for d in (1, 2, 3)]
    for peer in peers:
        pl.semaphore_signal(barrier, inc=1, device_id=peer, device_id_type=MESH)

    for load in loads[:3]:
        load.wait()
    loads[3].start()
    base = jnp.transpose(jnp.broadcast_to(base_row[...], (tokens, tokens)))
    mixed_seed = seed_ref[0] * jnp.int32(1013904223)
    first = col * ff

    def round_rows(j, count):
        rows = slice(j * block, (j + count) * block)

        def round_columns(n, _):
            columns = pl.ds(pl.multiple_of(n * 128, 128), 128)
            counter = base[rows] + (first + n * 128 + lax.broadcasted_iota(jnp.int32, (count * block, 128), 1))
            mixed = counter * jnp.int32(747796405) + mixed_seed
            mixed = mixed ^ (mixed >> 15)
            mixed = mixed * jnp.int32(277803737)
            mixed = mixed ^ (mixed >> 16)
            level = (mixed & 255).astype(jnp.float32)
            scaled = grad[rows, columns].astype(jnp.float32) * 4.0 + (level + 0.5) / 256.0
            rounded = (jnp.floor(scaled) / 4.0).astype(jnp.bfloat16)
            g_ref[x, lo, pl.ds(j, count), :, columns] = rounded.reshape(count, block, 128)
            return 0

        lax.fori_loop(0, ff // 128, round_columns, 0)

    round_rows(0, 1)
    pl.semaphore_wait(barrier, len(peers))

    sends = []

    def send_g(i, j, to):
        where = g_ref.at[root(i), lo_of(i), j]
        copy = remote(where, where, gs.at[len(sends)], gr.at[root(i), lo_of(i), j], to)
        copy.start()
        sends.append(copy)

    def wait_g(i, *js):
        for j in js:
            where = g_ref.at[root(i), lo_of(i), j]
            remote(where, where, gs.at[0], gr.at[root(i), lo_of(i), j], here).wait_recv()

    def half_chunk(i, half):
        return g_ref.at[root(i), lo_of(i), 3, pl.ds(half * (block // 2), block // 2)]

    def send_half(i, half, to):
        copy = remote(half_chunk(i, half), half_chunk(i, half), gs.at[len(sends)], hr.at[half], to)
        copy.start()
        sends.append(copy)

    def wait_half(half):
        where = half_chunk(FAR2, half)
        remote(where, where, gs.at[0], hr.at[half], here).wait_recv()

    def core_copy(i, q):
        return remote(part.at[i, q, 1 - core], crecv.at[i, q], cs.at[i, q], cr.at[i, q], sibling)

    def project(*pieces):
        left_side = jnp.concatenate(
            [g_ref[root(i), lo_of(i), pl.ds(j, n)].reshape(n * block, ff) for i, j, n in pieces], axis=0
        )
        value = lax.dot_general(
            left_side, turned[...], (((1,), (0,)), ((), ())), preferred_element_type=jnp.float32
        ).astype(jnp.bfloat16)
        row = 0
        for i, j, n in pieces:
            for k in range(j, j + n):
                part[i, k // 2, k % 2] = value[row : row + block]
                row += block

    def send_core(*units):
        for i, q in units:
            core_copy(i, q).start()

    def y_copy(i, q):
        k = lax.rem(y + NY - root(i), NY) - 1
        return remote(ssum.at[i, q], yrecv.at[lo_of(i), k, q], ys.at[i, q], yr.at[lo_of(i), k, q], at_y(root(i)))

    def add_cores(*units):
        for i, q in units:
            core_copy(i, q).wait_recv()
            ssum[i, q] = (part[i, q, core].astype(jnp.float32) + crecv[i, q].astype(jnp.float32)).astype(jnp.bfloat16)

            @pl.when(y != root(i))
            def _():
                y_copy(i, q).start()

    def z_copy(q):
        to = 2 * (1 - lo) + q
        k = lax.rem(hi + NH - to, NH) - 1
        return remote(tsum.at[1 - lo, q], zrecv.at[k], zs.at[q], zr.at[k], at_hi(to))

    def sum_columns(i, q):
        lo_root = lo_of(i)
        total = ssum[i, q].astype(jnp.float32)
        for k in range(3):
            where = yrecv.at[lo_root, k, q]
            remote(where, where, ys.at[i, q], yr.at[lo_root, k, q], here).wait_recv()
            total += yrecv[lo_root, k, q].astype(jnp.float32)
        tsum[lo_root, q] = total.astype(jnp.bfloat16)

    def add_columns(*units):
        for i, q in units:

            @pl.when(y == root(i))
            def _():
                sum_columns(i, q)

                @pl.when(hi != 2 * (1 - lo) + q)
                def _():
                    z_copy(q).start()

    parity = lax.rem(hi, 2)
    far = lax.rem(lax.div(hi, 2) + lo, 2)
    keep = lax.rem(parity + far, 2)

    def pair_copy():
        return remote(tsum.at[lo, 1 - keep], zpair, ts.at[0], tr.at[0], at_hi(hi + 1 - 2 * parity))

    def far_copy():
        return remote(tsum.at[lo, keep], zfar, ts.at[1], tr.at[1], at_hi(lax.rem(hi + 3 - 2 * parity, NH)))

    def add_plane(*shards):
        for i in shards:

            @pl.when(y == root(i))
            def _():
                for q in range(2):
                    sum_columns(i, q)
                pair_copy().start()

    def pass_on():
        remote(zpair, zpair, ts.at[0], tr.at[0], here).wait_recv()

        @pl.when(far == 1)
        def _():
            tsum[lo, keep] = (tsum[lo, keep].astype(jnp.float32) + zpair[...].astype(jnp.float32)).astype(jnp.bfloat16)
            far_copy().start()

    def az_copy(d):
        where = a_ref.at[y, hi, core]
        return remote(where, where, azs.at[d - 1], azr.at[d - 1], at_hi(lax.rem(hi + d, NH)))

    def az_wait(d):
        where = a_ref.at[y, lax.rem(hi + NH - d, NH), core]
        remote(where, where, azs.at[d - 1], azr.at[d - 1], here).wait_recv()

    def ay_copy(n):
        up, down = lax.rem(y + 1, NY), lax.rem(y + NY - 1, NY)
        owner, half, to, k = ((y, 0, up, 0), (y, 1, down, 2), (y, 1, up, 0), (y, 0, down, 2), (down, 0, up, 1), (up, 1, down, 1))[n]
        where = a_ref.at[owner, pl.ds(2 * half, 2), core]
        return remote(where, where, ays.at[n], ayr.at[k, half], at_y(to))

    def ay_wait(d, half):
        where = a_ref.at[lax.rem(y + NY - d, NY), pl.ds(2 * half, 2), core]
        remote(where, where, ays.at[0], ayr.at[d - 1, half], here).wait_recv()

    def ac_copy(d):
        where = a_ref.at[lax.rem(y + NY - d, NY), :, core]
        return remote(where, where, acs.at[d], acr.at[d], sibling)

    def ac_wait(d):
        where = a_ref.at[lax.rem(y + NY - d, NY), :, 1 - core]
        remote(where, where, acs.at[d], acr.at[d], here).wait_recv()

    def turn_act(plane):
        for r in range(NX):
            rows = a_ref[r, pl.ds(2 * plane, 2)].reshape(tokens, features)
            turned_act[:, r * tokens : (r + 1) * tokens] = jnp.transpose(rows)

    def accumulate(plane, span, last):
        lowest, highest = span
        value = lax.dot_general(
            turned_act[...],
            g_ref[:, plane, :, :, lowest:highest].reshape(NX * tokens, highest - lowest),
            (((1,), (0,)), ((), ())),
            preferred_element_type=jnp.float32,
        )
        if last:
            value = (total_ref[:, lowest:highest] + value) * (NX * 2 * tokens) ** (-0.5)
        total_ref[:, lowest:highest] = value

    spans = [(n, min(n + 512, ff)) for n in range(0, ff, 512)]

    for d in (1, 2, 3):
        az_copy(d).start()
    send_g(OWN, 0, right)
    round_rows(1, 1)
    send_g(OWN, 1, left)
    round_rows(2, 2)
    send_g(OWN, 3, pair)
    send_g(OWN, 0, pair)
    for j, k in ((2, 3), (1, 0), (3, 2)):
        send_g(OWN, j, right)
        send_g(OWN, k, left)
    send_g(OWN, 1, pair)
    send_g(OWN, 2, pair)
    loads[3].wait()

    def turn_weight(n, _):
        some = pl.ds(pl.multiple_of(n * 128, 128), 128)
        turned[:, some] = jnp.transpose(weight[some, :])
        return 0

    lax.fori_loop(0, features // 128, turn_weight, 0)
    project((OWN, 0, 4))
    send_core((OWN, 0), (OWN, 1))
    wait_g(LEFT, 0)
    send_g(LEFT, 0, right)
    wait_g(RIGHT, 1)
    send_g(RIGHT, 1, left)
    add_cores((OWN, 0), (OWN, 1))
    wait_g(LEFT, 2)
    send_g(LEFT, 2, right)
    wait_g(RIGHT, 3)
    send_g(RIGHT, 3, left)
    for d in (1, 2, 3):
        az_wait(d)
    for n in range(4):
        ay_copy(n).start()
    ac_copy(0).start()
    wait_g(OWN2, 3)
    send_g(OWN2, 3, right)
    send_g(OWN2, 3, left)
    wait_g(LEFT, 1, 3)
    wait_g(RIGHT, 0, 2)
    project((LEFT, 0, 4), (RIGHT, 0, 4))
    send_core((LEFT, 0), (LEFT, 1), (RIGHT, 0), (RIGHT, 1))
    wait_g(OWN2, 0)
    send_g(OWN2, 0, right)
    send_g(OWN2, 0, left)
    wait_g(FAR, 0, 1)
    send_g(FAR, 0, pair)
    send_g(FAR, 1, pair)
    ay_wait(1, 0)
    ay_copy(4).start()
    ay_wait(3, 1)
    ay_copy(5).start()
    wait_g(OWN2, 1)
    send_g(OWN2, 1, right)
    send_g(OWN2, 1, left)
    add_cores((LEFT, 0), (LEFT, 1), (RIGHT, 0), (RIGHT, 1))
    wait_g(FAR, 2, 3)
    send_g(FAR, 2, pair)
    wait_g(OWN2, 2)
    project((FAR, 0, 4), (OWN2, 0, 4))
    send_core((FAR, 0), (FAR, 1), (OWN2, 0), (OWN2, 1))
    wait_g(LEFT2, 3)
    send_half(LEFT2, 0, right)
    send_g(OWN2, 2, right)
    wait_g(RIGHT2, 3)
    send_half(RIGHT2, 1, left)
    send_g(OWN2, 2, left)
    add_plane(OWN)
    ay_wait(1, 1)
    ac_copy(1).start()
    ay_wait(3, 0)
    ac_copy(3).start()
    add_cores((FAR, 0), (FAR, 1), (OWN2, 0), (OWN2, 1))
    wait_g(LEFT2, 0)
    wait_g(RIGHT2, 0)
    wait_g(FAR2, 0)
    project((LEFT2, 3, 1), (RIGHT2, 3, 1), (LEFT2, 0, 1), (RIGHT2, 0, 1), (FAR2, 0, 1))

    @pl.when(core == 0)
    def _():
        send_core((LEFT2, 1), (RIGHT2, 1))

    @pl.when(core == 1)
    def _():
        send_core((FAR2, 0), (LEFT2, 0), (RIGHT2, 0))

    ay_wait(2, 0)
    ay_wait(2, 1)
    ac_copy(2).start()
    wait_g(LEFT2, 1)
    wait_g(RIGHT2, 1)
    wait_g(FAR2, 1)
    project((LEFT2, 1, 1), (RIGHT2, 1, 1), (FAR2, 1, 1))

    @pl.when(core == 0)
    def _():
        send_core((FAR2, 0), (LEFT2, 0), (RIGHT2, 0))
        add_cores((FAR2, 0), (LEFT2, 0), (RIGHT2, 0))

    @pl.when(core == 1)
    def _():
        add_cores((LEFT2, 1), (RIGHT2, 1))

    wait_half(0)
    wait_half(1)
    project((FAR2, 3, 1))

    @pl.when(core == 0)
    def _():
        send_core((FAR2, 1))

    wait_g(LEFT2, 2)
    wait_g(RIGHT2, 2)
    wait_g(FAR2, 2)
    project((LEFT2, 2, 1), (RIGHT2, 2, 1), (FAR2, 2, 1))

    @pl.when(core == 1)
    def _():
        send_core((FAR2, 1), (LEFT2, 1), (RIGHT2, 1))

    for d in range(4):
        ac_wait(d)
    turn_act(lo)

    @pl.when(core == 1)
    def _():
        add_cores((FAR2, 0), (LEFT2, 0), (RIGHT2, 0), (FAR2, 1))

    add_plane(FAR, LEFT, RIGHT)

    @pl.when(core == 0)
    def _():
        add_cores((FAR2, 1), (LEFT2, 1), (RIGHT2, 1))

    accumulate(lo, spans[0], False)
    add_columns((OWN2, 0), (OWN2, 1))

    @pl.when(core == 1)
    def _():
        add_columns((LEFT2, 1), (RIGHT2, 1))

    accumulate(lo, spans[1], False)
    add_columns((FAR2, 0), (LEFT2, 0), (RIGHT2, 0))
    for span in spans[2:]:
        accumulate(lo, span, False)

    @pl.when(core == 0)
    def _():
        add_columns((FAR2, 1), (LEFT2, 1), (RIGHT2, 1))

    @pl.when(core == 1)
    def _():
        add_columns((FAR2, 1))

    pass_on()
    turn_act(1 - lo)
    for span in spans:
        accumulate(1 - lo, span, True)

    total = tsum[lax.div(hi, 2), parity].astype(jnp.float32)

    @pl.when(far == 0)
    def _():
        remote(zfar, zfar, ts.at[1], tr.at[1], here).wait_recv()
        out_ref[...] = (total + zpair[...].astype(jnp.float32) + zfar[...].astype(jnp.float32)).astype(jnp.bfloat16)

    @pl.when(far == 1)
    def _():
        for k in range(3):
            remote(zrecv.at[k], zrecv.at[k], zs.at[0], zr.at[k], here).wait_recv()
        rest = sum(zrecv[k].astype(jnp.float32) for k in range(3))
        out_ref[...] = (total + rest).astype(jnp.bfloat16)

    for copy in sends:
        copy.wait_send()
    for i in range(8):
        for q in range(2):
            core_copy(i, q).wait_send()

            @pl.when(y != root(i))
            def _():
                y_copy(i, q).wait_send()

    for q in range(2):

        @pl.when(hi != 2 * (1 - lo) + q)
        def _():
            z_copy(q).wait_send()

    pair_copy().wait_send()

    @pl.when(far == 1)
    def _():
        far_copy().wait_send()

    for d in (1, 2, 3):
        az_copy(d).wait_send()
    for n in range(6):
        ay_copy(n).wait_send()
    for d in range(4):
        ac_copy(d).wait_send()


def store_kernel(total_ref, rows_ref, total_hbm, rows_hbm, sem):
    pieces = 8
    step = total_ref.shape[0] // pieces
    copies = [pltpu.make_async_copy(rows_ref, rows_hbm, sem.at[pieces])]
    for n in range(pieces):
        some = pl.ds(n * step, step)
        copies.append(pltpu.make_async_copy(total_ref.at[some], total_hbm.at[some], sem.at[n]))
    for copy in copies:
        copy.start()
    for copy in copies:
        copy.wait()


def shards(activations, up_weight, out_grad, round_seed, counter_base):
    tokens, ff = out_grad.shape
    few, features = activations.shape
    bf16, f32, dma = jnp.bfloat16, jnp.float32, pltpu.SemaphoreType.DMA
    vmem, hbm = pl.BlockSpec(memory_space=pltpu.VMEM), pl.BlockSpec(memory_space=pltpu.HBM)
    operands = (activations, up_weight, out_grad, counter_base.reshape(1, tokens))
    held = [pltpu.with_memory_space_constraint(v, pltpu.HBM) for v in operands]
    total, input_rows = pl.pallas_call(
        exchange_kernel,
        out_shape=(pltpu.VMEM((features, ff), f32), pltpu.VMEM((few, features), bf16)),
        in_specs=[hbm] * 4 + [pl.BlockSpec(memory_space=pltpu.SMEM)],
        out_specs=(vmem, vmem),
        scratch_shapes=[
            pltpu.VMEM((NX, 2, 4, tokens // 4, ff), bf16),
            pltpu.VMEM((NY, NH, 2, few, features), bf16),
            pltpu.VMEM((tokens, ff), bf16),
            pltpu.VMEM((features, ff), bf16),
            pltpu.VMEM((ff, features), bf16),
            pltpu.VMEM((features, NX * tokens), bf16),
            pltpu.VMEM((1, tokens), jnp.int32),
            pltpu.VMEM((8, 2, 2, few, features), bf16),
            pltpu.VMEM((8, 2, few, features), bf16),
            pltpu.VMEM((8, 2, few, features), bf16),
            pltpu.VMEM((2, 3, 2, few, features), bf16),
            pltpu.VMEM((2, 2, few, features), bf16),
            pltpu.VMEM((3, few, features), bf16),
            pltpu.VMEM((few, features), bf16),
            pltpu.VMEM((few, features), bf16),
            dma((4,)), dma((29,)), dma((NX, 2, 4)), dma((2,)), dma((8, 2)), dma((8, 2)), dma((8, 2)), dma((2, 3, 2)),
            dma((2,)), dma((3,)), dma((2,)), dma((2,)), dma((3,)), dma((3,)), dma((6,)), dma((3, 2)), dma((4,)), dma((4,)),
        ],
        compiler_params=pltpu.CompilerParams(
            collective_id=0, has_side_effects=True, vmem_limit_bytes=48 * 1024 * 1024
        ),
        name="exchange",
    )(*held, round_seed)
    total, input_rows = (pltpu.with_memory_space_constraint(v, pltpu.VMEM) for v in (total, input_rows))
    return pl.pallas_call(
        store_kernel,
        out_shape=(jax.ShapeDtypeStruct((features, ff), f32), jax.ShapeDtypeStruct((few, features), bf16)),
        in_specs=[vmem, vmem],
        out_specs=(hbm, hbm),
        scratch_shapes=[dma((9,))],
        compiler_params=pltpu.CompilerParams(vmem_limit_bytes=4 * 1024 * 1024),
        name="store",
    )(total, input_rows)


def solution(mesh):
    placed = (P("col", "row"), P("row", "col"), P("row", "col"), P(), P("row"))
    return jax.shard_map(
        shards,
        mesh=mesh,
        in_specs=placed,
        out_specs=(P("row", "col"), P("col", "row")),
        check_vma=False,
    )
```

```python
import jax
import jax.numpy as jnp
from jax import lax
from jax.experimental import pallas as pl
from jax.experimental.pallas import tpu as pltpu
from jax.sharding import PartitionSpec as P

MESH = pl.DeviceIdType.MESH
NX, NY, NH = 4, 4, 4
OWN, LEFT, RIGHT, FAR, OWN2, LEFT2, RIGHT2, FAR2 = range(8)
SHARDS = ((0, 0), (3, 0), (1, 0), (2, 0), (0, 1), (3, 1), (1, 1), (2, 1))


def device(x, lo, y, hi, core):
    return (x * 2 + lo, (y * NH + hi) * 2 + core)


def exchange_kernel(
    act_hbm, weight_hbm, grad_hbm, base_hbm, seed_ref, total_ref, out_ref,
    g_ref, a_ref, grad, weight, turned, turned_act, base_row, part, crecv, ssum, yrecv, tsum, zrecv, zpair, zfar,
    lsem, gs, gr, hr, cs, cr, ys, yr, zs, zr, ts, tr, azs, azr, ays, ayr, acs, acr,
):
    row, col = lax.axis_index("row"), lax.axis_index("col")
    x, lo = lax.div(row, 2), lax.rem(row, 2)
    y, hi, core = lax.div(col, 8), lax.rem(lax.div(col, 2), 4), lax.rem(col, 2)
    tokens, ff = grad.shape
    features = weight.shape[0]
    block = tokens // 4
    here = device(x, lo, y, hi, core)
    right = device(lax.rem(x + 1, NX), lo, y, hi, core)
    left = device(lax.rem(x + 3, NX), lo, y, hi, core)
    pair = device(x, 1 - lo, y, hi, core)
    sibling = device(x, lo, y, hi, 1 - core)

    def at_y(yy):
        return device(x, lo, yy, hi, core)

    def at_hi(hh):
        return device(x, lo, y, hh, core)

    def lo_of(i):
        return lax.rem(lo + SHARDS[i][1], 2)

    def root(i):
        return lax.rem(x + SHARDS[i][0], NX)


    def remote(src, dst, send, recv, to):
        return pltpu.make_async_remote_copy(
            src_ref=src, dst_ref=dst, send_sem=send, recv_sem=recv, device_id=to, device_id_type=MESH
        )

    loads = [
        pltpu.make_async_copy(base_hbm, base_row, lsem.at[0]),
        pltpu.make_async_copy(grad_hbm, grad, lsem.at[1]),
        pltpu.make_async_copy(act_hbm, a_ref.at[y, hi, core], lsem.at[2]),
        pltpu.make_async_copy(weight_hbm, weight, lsem.at[3]),
    ]
    for load in loads[:3]:
        load.start()

    barrier = pltpu.get_barrier_semaphore()
    peers = [right, left, pair, sibling]
    peers += [at_y(lax.rem(y + d, NY)) for d in (1, 2, 3)]
    peers += [at_hi(lax.rem(hi + d, NH)) for d in (1, 2, 3)]
    for peer in peers:
        pl.semaphore_signal(barrier, inc=1, device_id=peer, device_id_type=MESH)

    for load in loads[:3]:
        load.wait()
    loads[3].start()
    base = jnp.transpose(jnp.broadcast_to(base_row[...], (tokens, tokens)))
    mixed_seed = seed_ref[0] * jnp.int32(1013904223)
    first = col * ff

    def round_rows(j, count):
        rows = slice(j * block, (j + count) * block)

        def round_columns(n, _):
            columns = pl.ds(pl.multiple_of(n * 128, 128), 128)
            counter = base[rows] + (first + n * 128 + lax.broadcasted_iota(jnp.int32, (count * block, 128), 1))
            mixed = counter * jnp.int32(747796405) + mixed_seed
            mixed = mixed ^ (mixed >> 15)
            mixed = mixed * jnp.int32(277803737)
            mixed = mixed ^ (mixed >> 16)
            level = (mixed & 255).astype(jnp.float32)
            scaled = grad[rows, columns].astype(jnp.float32) * 4.0 + (level + 0.5) / 256.0
            rounded = (jnp.floor(scaled) / 4.0).astype(jnp.bfloat16)
            g_ref[x, lo, pl.ds(j, count), :, columns] = rounded.reshape(count, block, 128)
            return 0

        lax.fori_loop(0, ff // 128, round_columns, 0)

    round_rows(0, 1)
    pl.semaphore_wait(barrier, len(peers))

    sends = []

    def send_g(i, j, to):
        where = g_ref.at[root(i), lo_of(i), j]
        copy = remote(where, where, gs.at[len(sends)], gr.at[root(i), lo_of(i), j], to)
        copy.start()
        sends.append(copy)

    def wait_g(i, *js):
        for j in js:
            where = g_ref.at[root(i), lo_of(i), j]
            remote(where, where, gs.at[0], gr.at[root(i), lo_of(i), j], here).wait_recv()

    def half_chunk(i, half):
        return g_ref.at[root(i), lo_of(i), 3, pl.ds(half * (block // 2), block // 2)]

    def send_half(i, half, to):
        copy = remote(half_chunk(i, half), half_chunk(i, half), gs.at[len(sends)], hr.at[half], to)
        copy.start()
        sends.append(copy)

    def wait_half(half):
        where = half_chunk(FAR2, half)
        remote(where, where, gs.at[0], hr.at[half], here).wait_recv()

    def core_copy(i, q):
        return remote(part.at[i, q, 1 - core], crecv.at[i, q], cs.at[i, q], cr.at[i, q], sibling)

    def project(*pieces):
        left_side = jnp.concatenate(
            [g_ref[root(i), lo_of(i), pl.ds(j, n)].reshape(n * block, ff) for i, j, n in pieces], axis=0
        )
        value = lax.dot_general(
            left_side, turned[...], (((1,), (0,)), ((), ())), preferred_element_type=jnp.float32
        ).astype(jnp.bfloat16)
        row = 0
        for i, j, n in pieces:
            for k in range(j, j + n):
                part[i, k // 2, k % 2] = value[row : row + block]
                row += block

    def send_core(*units):
        for i, q in units:
            core_copy(i, q).start()

    def y_copy(i, q):
        k = lax.rem(y + NY - root(i), NY) - 1
        return remote(ssum.at[i, q], yrecv.at[lo_of(i), k, q], ys.at[i, q], yr.at[lo_of(i), k, q], at_y(root(i)))

    def add_cores(*units):
        for i, q in units:
            core_copy(i, q).wait_recv()
            ssum[i, q] = (part[i, q, core].astype(jnp.float32) + crecv[i, q].astype(jnp.float32)).astype(jnp.bfloat16)

            @pl.when(y != root(i))
            def _():
                y_copy(i, q).start()

    def z_copy(q):
        to = 2 * (1 - lo) + q
        k = lax.rem(hi + NH - to, NH) - 1
        return remote(tsum.at[1 - lo, q], zrecv.at[k], zs.at[q], zr.at[k], at_hi(to))

    def sum_columns(i, q):
        lo_root = lo_of(i)
        total = ssum[i, q].astype(jnp.float32)
        for k in range(3):
            where = yrecv.at[lo_root, k, q]
            remote(where, where, ys.at[i, q], yr.at[lo_root, k, q], here).wait_recv()
            total += yrecv[lo_root, k, q].astype(jnp.float32)
        tsum[lo_root, q] = total.astype(jnp.bfloat16)

    def add_columns(*units):
        for i, q in units:

            @pl.when(y == root(i))
            def _():
                sum_columns(i, q)

                @pl.when(hi != 2 * (1 - lo) + q)
                def _():
                    z_copy(q).start()

    parity = lax.rem(hi, 2)
    far = lax.rem(lax.div(hi, 2) + lo, 2)
    keep = lax.rem(parity + far, 2)

    def pair_copy():
        return remote(tsum.at[lo, 1 - keep], zpair, ts.at[0], tr.at[0], at_hi(hi + 1 - 2 * parity))

    def far_copy():
        return remote(tsum.at[lo, keep], zfar, ts.at[1], tr.at[1], at_hi(lax.rem(hi + 3 - 2 * parity, NH)))

    def add_plane(*shards):
        for i in shards:

            @pl.when(y == root(i))
            def _():
                for q in range(2):
                    sum_columns(i, q)
                pair_copy().start()

    def pass_on():
        remote(zpair, zpair, ts.at[0], tr.at[0], here).wait_recv()

        @pl.when(far == 1)
        def _():
            tsum[lo, keep] = (tsum[lo, keep].astype(jnp.float32) + zpair[...].astype(jnp.float32)).astype(jnp.bfloat16)
            far_copy().start()

    def az_copy(d):
        where = a_ref.at[y, hi, core]
        return remote(where, where, azs.at[d - 1], azr.at[d - 1], at_hi(lax.rem(hi + d, NH)))

    def az_wait(d):
        where = a_ref.at[y, lax.rem(hi + NH - d, NH), core]
        remote(where, where, azs.at[d - 1], azr.at[d - 1], here).wait_recv()

    def ay_copy(n):
        up, down = lax.rem(y + 1, NY), lax.rem(y + NY - 1, NY)
        owner, half, to, k = ((y, 0, up, 0), (y, 1, down, 2), (y, 1, up, 0), (y, 0, down, 2), (down, 0, up, 1), (up, 1, down, 1))[n]
        where = a_ref.at[owner, pl.ds(2 * half, 2), core]
        return remote(where, where, ays.at[n], ayr.at[k, half], at_y(to))

    def ay_wait(d, half):
        where = a_ref.at[lax.rem(y + NY - d, NY), pl.ds(2 * half, 2), core]
        remote(where, where, ays.at[0], ayr.at[d - 1, half], here).wait_recv()

    def ac_copy(d):
        where = a_ref.at[lax.rem(y + NY - d, NY), :, core]
        return remote(where, where, acs.at[d], acr.at[d], sibling)

    def ac_wait(d):
        where = a_ref.at[lax.rem(y + NY - d, NY), :, 1 - core]
        remote(where, where, acs.at[d], acr.at[d], here).wait_recv()

    def turn_act(plane):
        for r in range(NX):
            rows = a_ref[r, pl.ds(2 * plane, 2)].reshape(tokens, features)
            turned_act[:, r * tokens : (r + 1) * tokens] = jnp.transpose(rows)

    def accumulate(plane, span, last):
        lowest, highest = span
        value = lax.dot_general(
            turned_act[...],
            g_ref[:, plane, :, :, lowest:highest].reshape(NX * tokens, highest - lowest),
            (((1,), (0,)), ((), ())),
            preferred_element_type=jnp.float32,
        )
        if last:
            value = (total_ref[:, lowest:highest] + value) * (NX * 2 * tokens) ** (-0.5)
        total_ref[:, lowest:highest] = value

    spans = [(n, min(n + 512, ff)) for n in range(0, ff, 512)]

    for d in (1, 2, 3):
        az_copy(d).start()
    send_g(OWN, 0, right)
    round_rows(1, 1)
    send_g(OWN, 1, left)
    round_rows(2, 2)
    for j, k in ((2, 3), (1, 0), (3, 2)):
        send_g(OWN, j, right)
        send_g(OWN, k, left)
    loads[3].wait()

    def turn_weight(n, _):
        some = pl.ds(pl.multiple_of(n * 128, 128), 128)
        turned[:, some] = jnp.transpose(weight[some, :])
        return 0

    lax.fori_loop(0, features // 128, turn_weight, 0)
    for j in (3, 0, 1, 2):
        send_g(OWN, j, pair)
    project((OWN, 0, 4))
    send_core((OWN, 0), (OWN, 1))
    wait_g(LEFT, 0)
    send_g(LEFT, 0, right)
    wait_g(RIGHT, 1)
    send_g(RIGHT, 1, left)
    add_cores((OWN, 0), (OWN, 1))
    wait_g(LEFT, 2)
    send_g(LEFT, 2, right)
    wait_g(RIGHT, 3)
    send_g(RIGHT, 3, left)
    for d in (1, 2, 3):
        az_wait(d)
    for n in range(4):
        ay_copy(n).start()
    ac_copy(0).start()
    wait_g(OWN2, 3)
    send_g(OWN2, 3, right)
    send_g(OWN2, 3, left)
    wait_g(LEFT, 1, 3)
    wait_g(RIGHT, 0, 2)
    project((LEFT, 0, 4), (RIGHT, 0, 4))
    send_core((LEFT, 0), (LEFT, 1), (RIGHT, 0), (RIGHT, 1))
    wait_g(OWN2, 0)
    send_g(OWN2, 0, right)
    send_g(OWN2, 0, left)
    wait_g(FAR, 0, 1)
    send_g(FAR, 0, pair)
    send_g(FAR, 1, pair)
    ay_wait(1, 0)
    ay_copy(4).start()
    ay_wait(3, 1)
    ay_copy(5).start()
    wait_g(OWN2, 1)
    send_g(OWN2, 1, right)
    send_g(OWN2, 1, left)
    add_cores((LEFT, 0), (LEFT, 1), (RIGHT, 0), (RIGHT, 1))
    wait_g(FAR, 2, 3)
    send_g(FAR, 2, pair)
    project((FAR, 0, 4))
    send_core((FAR, 0), (FAR, 1))
    wait_g(OWN2, 2)
    project((OWN2, 0, 4))
    send_core((OWN2, 0), (OWN2, 1))
    wait_g(LEFT2, 3)
    send_half(LEFT2, 0, right)
    send_g(OWN2, 2, right)
    wait_g(RIGHT2, 3)
    send_half(RIGHT2, 1, left)
    send_g(OWN2, 2, left)
    add_plane(OWN)
    ay_wait(1, 1)
    ac_copy(1).start()
    ay_wait(3, 0)
    ac_copy(3).start()
    add_cores((FAR, 0), (FAR, 1), (OWN2, 0), (OWN2, 1))
    wait_g(LEFT2, 0)
    wait_g(RIGHT2, 0)
    wait_g(FAR2, 0)
    project((LEFT2, 3, 1), (RIGHT2, 3, 1), (LEFT2, 0, 1), (RIGHT2, 0, 1), (FAR2, 0, 1))

    @pl.when(core == 0)
    def _():
        send_core((LEFT2, 1), (RIGHT2, 1))

    @pl.when(core == 1)
    def _():
        send_core((FAR2, 0), (LEFT2, 0), (RIGHT2, 0))

    ay_wait(2, 0)
    ay_wait(2, 1)
    ac_copy(2).start()
    wait_g(LEFT2, 1)
    wait_g(RIGHT2, 1)
    wait_g(FAR2, 1)
    project((LEFT2, 1, 1), (RIGHT2, 1, 1), (FAR2, 1, 1))

    @pl.when(core == 0)
    def _():
        send_core((FAR2, 0), (LEFT2, 0), (RIGHT2, 0))
        add_cores((FAR2, 0), (LEFT2, 0), (RIGHT2, 0))

    @pl.when(core == 1)
    def _():
        add_cores((LEFT2, 1), (RIGHT2, 1))

    wait_half(0)
    wait_half(1)
    project((FAR2, 3, 1))

    @pl.when(core == 0)
    def _():
        send_core((FAR2, 1))

    wait_g(LEFT2, 2)
    wait_g(RIGHT2, 2)
    wait_g(FAR2, 2)
    project((LEFT2, 2, 1), (RIGHT2, 2, 1), (FAR2, 2, 1))

    @pl.when(core == 1)
    def _():
        send_core((FAR2, 1), (LEFT2, 1), (RIGHT2, 1))

    for d in range(4):
        ac_wait(d)
    turn_act(lo)

    @pl.when(core == 1)
    def _():
        add_cores((FAR2, 0), (LEFT2, 0), (RIGHT2, 0), (FAR2, 1))

    add_plane(FAR, LEFT, RIGHT)

    @pl.when(core == 0)
    def _():
        add_cores((FAR2, 1), (LEFT2, 1), (RIGHT2, 1))

    accumulate(lo, spans[0], False)
    add_columns((OWN2, 0), (OWN2, 1))

    @pl.when(core == 1)
    def _():
        add_columns((LEFT2, 1), (RIGHT2, 1))

    accumulate(lo, spans[1], False)
    add_columns((FAR2, 0), (LEFT2, 0), (RIGHT2, 0))
    for span in spans[2:]:
        accumulate(lo, span, False)

    @pl.when(core == 0)
    def _():
        add_columns((FAR2, 1), (LEFT2, 1), (RIGHT2, 1))

    @pl.when(core == 1)
    def _():
        add_columns((FAR2, 1))

    pass_on()
    turn_act(1 - lo)
    for span in spans:
        accumulate(1 - lo, span, True)

    total = tsum[lax.div(hi, 2), parity].astype(jnp.float32)

    @pl.when(far == 0)
    def _():
        remote(zfar, zfar, ts.at[1], tr.at[1], here).wait_recv()
        out_ref[...] = (total + zpair[...].astype(jnp.float32) + zfar[...].astype(jnp.float32)).astype(jnp.bfloat16)

    @pl.when(far == 1)
    def _():
        for k in range(3):
            remote(zrecv.at[k], zrecv.at[k], zs.at[0], zr.at[k], here).wait_recv()
        rest = sum(zrecv[k].astype(jnp.float32) for k in range(3))
        out_ref[...] = (total + rest).astype(jnp.bfloat16)

    for copy in sends:
        copy.wait_send()
    for i in range(8):
        for q in range(2):
            core_copy(i, q).wait_send()

            @pl.when(y != root(i))
            def _():
                y_copy(i, q).wait_send()

    for q in range(2):

        @pl.when(hi != 2 * (1 - lo) + q)
        def _():
            z_copy(q).wait_send()

    pair_copy().wait_send()

    @pl.when(far == 1)
    def _():
        far_copy().wait_send()

    for d in (1, 2, 3):
        az_copy(d).wait_send()
    for n in range(6):
        ay_copy(n).wait_send()
    for d in range(4):
        ac_copy(d).wait_send()


def store_kernel(total_ref, rows_ref, total_hbm, rows_hbm, sem):
    pieces = 8
    step = total_ref.shape[0] // pieces
    copies = [pltpu.make_async_copy(rows_ref, rows_hbm, sem.at[pieces])]
    for n in range(pieces):
        some = pl.ds(n * step, step)
        copies.append(pltpu.make_async_copy(total_ref.at[some], total_hbm.at[some], sem.at[n]))
    for copy in copies:
        copy.start()
    for copy in copies:
        copy.wait()


def shards(activations, up_weight, out_grad, round_seed, counter_base):
    tokens, ff = out_grad.shape
    few, features = activations.shape
    bf16, f32, dma = jnp.bfloat16, jnp.float32, pltpu.SemaphoreType.DMA
    vmem, hbm = pl.BlockSpec(memory_space=pltpu.VMEM), pl.BlockSpec(memory_space=pltpu.HBM)
    operands = (activations, up_weight, out_grad, counter_base.reshape(1, tokens))
    held = [pltpu.with_memory_space_constraint(v, pltpu.HBM) for v in operands]
    total, input_rows = pl.pallas_call(
        exchange_kernel,
        out_shape=(pltpu.VMEM((features, ff), f32), pltpu.VMEM((few, features), bf16)),
        in_specs=[hbm] * 4 + [pl.BlockSpec(memory_space=pltpu.SMEM)],
        out_specs=(vmem, vmem),
        scratch_shapes=[
            pltpu.VMEM((NX, 2, 4, tokens // 4, ff), bf16),
            pltpu.VMEM((NY, NH, 2, few, features), bf16),
            pltpu.VMEM((tokens, ff), bf16),
            pltpu.VMEM((features, ff), bf16),
            pltpu.VMEM((ff, features), bf16),
            pltpu.VMEM((features, NX * tokens), bf16),
            pltpu.VMEM((1, tokens), jnp.int32),
            pltpu.VMEM((8, 2, 2, few, features), bf16),
            pltpu.VMEM((8, 2, few, features), bf16),
            pltpu.VMEM((8, 2, few, features), bf16),
            pltpu.VMEM((2, 3, 2, few, features), bf16),
            pltpu.VMEM((2, 2, few, features), bf16),
            pltpu.VMEM((3, few, features), bf16),
            pltpu.VMEM((few, features), bf16),
            pltpu.VMEM((few, features), bf16),
            dma((4,)), dma((29,)), dma((NX, 2, 4)), dma((2,)), dma((8, 2)), dma((8, 2)), dma((8, 2)), dma((2, 3, 2)),
            dma((2,)), dma((3,)), dma((2,)), dma((2,)), dma((3,)), dma((3,)), dma((6,)), dma((3, 2)), dma((4,)), dma((4,)),
        ],
        compiler_params=pltpu.CompilerParams(
            collective_id=0, has_side_effects=True, vmem_limit_bytes=48 * 1024 * 1024
        ),
        name="exchange",
    )(*held, round_seed)
    total, input_rows = (pltpu.with_memory_space_constraint(v, pltpu.VMEM) for v in (total, input_rows))
    return pl.pallas_call(
        store_kernel,
        out_shape=(jax.ShapeDtypeStruct((features, ff), f32), jax.ShapeDtypeStruct((few, features), bf16)),
        in_specs=[vmem, vmem],
        out_specs=(hbm, hbm),
        scratch_shapes=[dma((9,))],
        compiler_params=pltpu.CompilerParams(vmem_limit_bytes=4 * 1024 * 1024),
        name="store",
    )(total, input_rows)


def solution(mesh):
    placed = (P("col", "row"), P("row", "col"), P("row", "col"), P(), P("row"))
    return jax.shard_map(
        shards,
        mesh=mesh,
        in_specs=placed,
        out_specs=(P("row", "col"), P("col", "row")),
        check_vma=False,
    )
```
